32 devices in a mesh: clip: 2 (over y), rows: 8 (over z, x), tm: 2 (over core).
Axes of the slice: x: 2, y: 2, z: 4, core: 2. Of those that a mesh axis runs over, the one named last changes fastest.
Arguments:
- latent: bfloat16 [8, 8, 64, 192], P(('clip', 'tm'), 'rows'), parts along dimension 0, may hold values from -18 to 18
- gain_first: bfloat16 [192], replicated, may hold values from 0.099609375 to 1.8984375
- conv_first: bfloat16 [3, 3, 3, 192, 192], replicated, may hold values from -0.078125 to 0.078125
- gain_second: bfloat16 [192], replicated, may hold values from 0.099609375 to 1.8984375
- conv_second: bfloat16 [3, 3, 3, 192, 192], replicated, may hold values from -0.078125 to 0.078125
- conv_up: bfloat16 [3, 3, 96, 192], replicated, may hold values from -0.15625 to 0.15625
Outputs:
- decoded: bfloat16 [8, 16, 96, 128], P(('clip', 'tm'), 'rows'), parts along dimension 0
- peaks: float32 [6, 192], P('clip'), parts along dimension 0
The draws below stay inside these ranges and needn't reach their ends.
There are 2 independent parts, one for each index of `clip`. The reference program is written for one: setup_inputs(seed, part) draws one part's arguments, and reference() takes and returns one part's arrays. A program takes and returns all parts, laid end to end along the dimension named above; an argument that names none is the same for every part. Nothing has to cross between parts.
All inputs are finite; a program needn't handle non-finite values.
Results may differ from the reference program's by a relative error of at most 0.0085.
Values may be sent and summed in bfloat16 or wider, within the bound.
No kernel may reach another device: no remote copies, remote signals or barrier semaphores. Data moves between devices by JAX's collectives and lax.ppermute only.
A program may use at most 64 MiB of HBM per device.

```python
import math
import jax
import jax.numpy as jnp
from jax import lax

C = 192
C2 = 96
COLS = 64
FRAMES = 4
ROWS = 8


def draw_latent(key, part):
    base_key = jax.random.fold_in(key, 11)
    noise_key, spread_key = jax.random.split(base_key)
    spread = jnp.exp(jax.random.uniform(spread_key, (1, ROWS, 1, C), jnp.float32, math.log(0.3), math.log(3.0)))
    rising = 0.5 + jnp.arange(ROWS, dtype=jnp.float32).reshape(1, ROWS, 1, 1) / ROWS
    noise = jnp.clip(jax.random.normal(noise_key, (FRAMES, ROWS, COLS, C), jnp.float32), -4.0, 4.0)
    return (noise * spread * rising).astype(jnp.bfloat16)


def scatter_about(own_key, dims, deviation, most, kind=jnp.bfloat16):
    entries = jax.random.normal(own_key, dims, jnp.float32) * deviation
    return jnp.minimum(jnp.maximum(entries, -most), most).astype(kind)


def setup_inputs(seed: int = 0, part: int = 0) -> dict:
    splits = jax.random.split(jax.random.key(seed), 7)
    part_splits = jax.random.split(jax.random.fold_in(splits[6], part), 7)
    latent = draw_latent(jax.random.fold_in(jax.random.fold_in(splits[6], part), 71), part)
    gain_first = jnp.clip(1.0 + 0.18 * jax.random.normal(splits[1], (C,), jnp.float32), 0.099609375, 1.8984375).astype(jnp.bfloat16)
    conv_first = scatter_about(splits[2], (3, 3, 3, C, C), (27 * C) ** -0.5, 0.078125)
    gain_second = jnp.clip(1.0 + 0.18 * jax.random.normal(splits[3], (C,), jnp.float32), 0.099609375, 1.8984375).astype(jnp.bfloat16)
    conv_second = scatter_about(splits[4], (3, 3, 3, C, C), (27 * C) ** -0.5, 0.078125)
    conv_up = scatter_about(splits[5], (3, 3, C2, C), (9 * C) ** -0.5, 0.15625)
    return {"latent": latent, "gain_first": gain_first, "conv_first": conv_first, "gain_second": gain_second, "conv_second": conv_second, "conv_up": conv_up}


def rms_norm(values, gain):
    floats = values.astype(jnp.float32)
    scale = lax.rsqrt(lax.optimization_barrier(jnp.mean(floats * floats, axis=-1, keepdims=True)) + 1e-06)
    return floats * scale * gain.astype(jnp.float32)

def causal_taps(extended, weights, frame_count, row_count, col_count):
    channels = extended.shape[-1]
    total = jnp.zeros((frame_count * row_count * col_count, weights.shape[-1]), jnp.float32)
    for time_tap in range(3):
        for row_tap in range(3):
            sliced = extended[time_tap:time_tap + frame_count, row_tap:row_tap + row_count]
            stacked = jnp.concatenate([sliced[:, :, col_tap:col_tap + col_count] for col_tap in range(3)], axis=-1)
            matrix = weights[time_tap, row_tap].reshape(3 * channels, weights.shape[-1])
            total = total + jnp.dot(stacked.reshape(-1, 3 * channels), matrix, preferred_element_type=jnp.float32)
    return total.reshape(frame_count, row_count, col_count, weights.shape[-1])

def plane_taps(wide_padded, conv_up, row_count, col_count):
    channels = wide_padded.shape[-1]
    frame_count = wide_padded.shape[0]
    total = jnp.zeros((frame_count * row_count * col_count, conv_up.shape[2]), jnp.float32)
    for row_tap in range(3):
        sliced = wide_padded[:, row_tap:row_tap + row_count]
        stacked = jnp.concatenate([sliced[:, :, col_tap:col_tap + col_count] for col_tap in range(3)], axis=-1)
        matrix = jnp.transpose(conv_up[row_tap], (0, 2, 1)).reshape(3 * channels, conv_up.shape[2])
        total = total + jnp.dot(stacked.reshape(-1, 3 * channels), matrix, preferred_element_type=jnp.float32)
    output = total.reshape(frame_count, row_count, col_count, conv_up.shape[2])
    return jnp.transpose(output, (0, 1, 3, 2)).astype(jnp.bfloat16)

def channel_peak(values):
    return lax.optimization_barrier(jnp.max(jnp.abs(values).astype(jnp.float32), axis=(0, 1, 2)))

def causal_whole(values, weights):
    frame_count, row_count, col_count = (values.shape[0], values.shape[1], values.shape[2])
    extended = jnp.pad(values, ((2, 0), (1, 1), (1, 1), (0, 0)))
    return causal_taps(extended, weights, frame_count, row_count, col_count)

def reference(latent, gain_first, conv_first, gain_second, conv_second, conv_up):
    first = jax.nn.silu(rms_norm(latent, gain_first)).astype(jnp.bfloat16)
    hidden = causal_whole(first, conv_first).astype(jnp.bfloat16)
    second = jax.nn.silu(rms_norm(hidden, gain_second)).astype(jnp.bfloat16)
    merged = (latent.astype(jnp.float32) + causal_whole(second, conv_second)).astype(jnp.bfloat16)
    row_count, col_count = (merged.shape[1], merged.shape[2])

    def one_frame(frame):
        wide = jnp.repeat(jnp.repeat(frame[None], 2, axis=1), 2, axis=2)
        wide = jnp.pad(wide, ((0, 0), (1, 1), (1, 1), (0, 0)))
        return plane_taps(wide, conv_up, 2 * row_count, 2 * col_count)[0]
    decoded = lax.map(one_frame, merged)
    peaks = jnp.stack([channel_peak(first), channel_peak(second), channel_peak(merged)], axis=0)
    return (decoded, peaks)
```

```python
import functools

import jax
import jax.numpy as jnp
from jax import lax
from jax.experimental import pallas as pl
from jax.experimental.pallas import tpu as pltpu
from jax.sharding import PartitionSpec as P


EPS = 1e-06
REACH = 3
VMEM = pl.BlockSpec(memory_space=pltpu.VMEM)


def swap_cores(block):
    return lax.ppermute(block, "tm", [(0, 1), (1, 0)])


def near_rows(block, distance):
    rows = lax.axis_size("rows")
    route = []
    for row in range(rows):
        down, up = row + distance, row - distance
        route.append((2 * row, 2 * down if down < rows else 2 * row + 1))
        route.append((2 * row + 1, 2 * up + 1 if up >= 0 else 2 * row))
    return lax.ppermute(block, ("rows", "tm"), route)


def half_silu(values, scale, half_gain):
    half = values * scale * half_gain
    return half + half * jnp.tanh(half)


def norm_plane(floats, half_gain, valid):
    scale = lax.rsqrt(jnp.mean(floats * floats, axis=-1, keepdims=True) + EPS)
    return half_silu(floats, scale * valid, half_gain)


def column_taps(plane):
    cols = plane.shape[0]
    col = lax.broadcasted_iota(jnp.int32, plane.shape, 0)
    left = jnp.where(col == 0, 0.0, pltpu.roll(plane, 1, 0))
    right = jnp.where(col == cols - 1, 0.0, pltpu.roll(plane, cols - 1, 0))
    return jnp.concatenate([left, plane, right], axis=-1).astype(jnp.bfloat16)


def store_taps(taps_ref, frame, row, taps, rows_out):
    width = taps.shape[-1]
    for row_tap in range(3):
        out = row - row_tap
        if 0 <= out < rows_out:
            taps_ref[frame, out, :, row_tap * width : (row_tap + 1) * width] = taps


def peak_of(plane):
    return jnp.max(jnp.abs(plane), axis=0, keepdims=True)


def block_kernel(
    own, near, far, gain_a, conv_a, gain_b, conv_b, merged, peaks, taps_a, taps_b, total_a, total_b
):
    frames, cols, channels = (merged.shape[0], merged.shape[2], merged.shape[3])
    rows = lax.axis_size("rows")
    row, core = lax.axis_index("rows"), lax.axis_index("tm")
    first_core = core == 0

    def latent_plane(offset, frame):
        own_frame = (frame + frames) % (2 * frames)
        if offset == 0:
            return own[own_frame, 0]
        step = abs(offset) - 1
        upper = first_core if offset < 0 else jnp.logical_not(first_core)
        return jnp.where(upper, near[step, own_frame, 0], far[step, frame, 0])

    def row_valid(offset):
        at = row + offset
        return jnp.where((at >= 0) & (at < rows), 1.0, 0.0)

    half_a = gain_a[...].astype(jnp.float32) * 0.5
    half_b = gain_b[...].astype(jnp.float32) * 0.5
    has_past = jnp.where(first_core, 0.0, 1.0)

    peak = jnp.zeros((1, channels), jnp.float32)
    for offset in range(-REACH, REACH + 1):
        for frame in range(2 * frames):
            valid = row_valid(offset)
            if frame < frames:
                valid = valid * has_past
            floats = latent_plane(offset, frame).astype(jnp.float32)
            first = norm_plane(floats, half_a, valid)
            if offset == 0 and frame >= frames:
                peak = jnp.maximum(peak, peak_of(first))
            store_taps(taps_a, frame, offset + REACH, column_taps(first), taps_a.shape[1])
    peaks[0:1] = peak.astype(jnp.bfloat16).astype(jnp.float32)

    def gathered(taps_ref, lower, upper):
        part = taps_ref[lower:upper]
        return part.reshape(-1, part.shape[-1])

    out_rows = taps_a.shape[1]
    plane = out_rows * cols
    for time_tap in (2, 1, 0):
        skip = 2 - time_tap
        count = 2 * frames - skip
        product = jnp.dot(
            gathered(taps_a, 0, count), conv_a[time_tap], preferred_element_type=jnp.float32
        )
        if skip == 0:
            total_a[...] = product
        else:
            total_a[skip * plane :] += product

    peak = jnp.zeros((1, channels), jnp.float32)
    for frame in range(2 * frames):
        for out in range(out_rows):
            offset = out - (REACH - 1)
            start = frame * plane + out * cols
            hidden = total_a[start : start + cols].astype(jnp.bfloat16).astype(jnp.float32)
            second = norm_plane(hidden, half_b, row_valid(offset))
            if offset == 0 and frame >= frames:
                peak = jnp.maximum(peak, peak_of(second))
            store_taps(taps_b, frame, out, column_taps(second), taps_b.shape[1])
    peaks[1:2] = peak.astype(jnp.bfloat16).astype(jnp.float32)

    for time_tap in (2, 1, 0):
        product = jnp.dot(
            gathered(taps_b, time_tap, time_tap + frames),
            conv_b[time_tap],
            preferred_element_type=jnp.float32,
        )
        if time_tap == 2:
            total_b[...] = product
        else:
            total_b[...] += product

    peak = jnp.zeros((1, channels), jnp.float32)
    out_rows = taps_b.shape[1]
    for frame in range(frames):
        for out in range(out_rows):
            offset = out - 1
            start = (frame * out_rows + out) * cols
            value = latent_plane(offset, frame + frames).astype(jnp.float32)
            value = (value + total_b[start : start + cols]) * row_valid(offset)
            merged[frame, out] = value.astype(jnp.bfloat16)
            if offset == 0:
                peak = jnp.maximum(peak, peak_of(value))
    peaks[2:3] = peak.astype(jnp.bfloat16).astype(jnp.float32)


def up_kernel(merged, conv_up, decoded):
    frames, _, cols, channels = merged.shape
    out_channels = conv_up.shape[2]
    wide_cols = 2 * cols
    spread = jnp.where(
        lax.broadcasted_iota(jnp.int32, (wide_cols, cols), 0) // 2
        == lax.broadcasted_iota(jnp.int32, (wide_cols, cols), 1),
        1.0,
        0.0,
    ).astype(jnp.bfloat16)
    col = lax.broadcasted_iota(jnp.int32, (out_channels, wide_cols), 1)
    contract = (((1,), (1,)), ((), ()))
    sources = ((0, 1, 1), (1, 1, 2))
    for frame in range(frames):
        wide = [
            jnp.dot(spread, merged[frame, at], preferred_element_type=jnp.float32).astype(
                jnp.bfloat16
            )
            for at in range(3)
        ]
        for half in range(2):
            sums = []
            for col_tap in range(3):
                total = None
                for row_tap in range(3):
                    term = lax.dot_general(
                        conv_up[row_tap, col_tap],
                        wide[sources[half][row_tap]],
                        contract,
                        preferred_element_type=jnp.float32,
                    )
                    total = term if total is None else total + term
                sums.append(total)
            left = jnp.where(col == 0, 0.0, pltpu.roll(sums[0], 1, 1))
            right = jnp.where(col == wide_cols - 1, 0.0, pltpu.roll(sums[2], wide_cols - 1, 1))
            decoded[frame, half] = (left + sums[1] + right).astype(jnp.bfloat16)


def group_peaks(peaks):
    rows = lax.axis_size("rows")
    bits = [1 << bit for bit in range(rows.bit_length() - 1)]
    while bits:
        now, bits = bits[:2], bits[2:]
        flips = now if len(now) == 1 else [now[0], now[1], now[0] | now[1]]
        arrived = [lax.ppermute(peaks, "rows", [(r, r ^ flip) for r in range(rows)]) for flip in flips]
        peaks = functools.reduce(jnp.maximum, arrived, peaks)
    return jnp.maximum(peaks, swap_cores(peaks))


def per_device(latent, gain_first, conv_first, gain_second, conv_second, conv_up):
    frames, _, cols, channels = latent.shape
    own = jnp.concatenate([latent, swap_cores(latent)], axis=0)
    near = jnp.stack([near_rows(own, distance) for distance in range(1, REACH + 1)])
    far = swap_cores(near)

    merged, peaks = pl.pallas_call(
        block_kernel,
        out_shape=(
            jax.ShapeDtypeStruct((frames, 3, cols, channels), jnp.bfloat16),
            jax.ShapeDtypeStruct((3, channels), jnp.float32),
        ),
        in_specs=[VMEM] * 7,
        out_specs=(VMEM, VMEM),
        scratch_shapes=[
            pltpu.VMEM((2 * frames, 5, cols, 9 * channels), jnp.bfloat16),
            pltpu.VMEM((2 * frames, 3, cols, 9 * channels), jnp.bfloat16),
            pltpu.VMEM((2 * frames * 5 * cols, channels), jnp.float32),
            pltpu.VMEM((frames * 3 * cols, channels), jnp.float32),
        ],
        compiler_params=pltpu.CompilerParams(vmem_limit_bytes=32 << 20),
        name="block",
    )(
        own,
        near,
        far,
        gain_first.reshape(1, channels),
        conv_first.reshape(3, 9 * channels, channels),
        gain_second.reshape(1, channels),
        conv_second.reshape(3, 9 * channels, channels),
    )
    peaks = group_peaks(peaks)
    decoded = pl.pallas_call(
        up_kernel,
        out_shape=jax.ShapeDtypeStruct((frames, 2, conv_up.shape[2], 2 * cols), jnp.bfloat16),
        in_specs=[VMEM] * 2,
        out_specs=VMEM,
        compiler_params=pltpu.CompilerParams(vmem_limit_bytes=16 << 20),
        cost_estimate=pl.CostEstimate(flops=200_000_000, bytes_accessed=1 << 20, transcendentals=0),
        name="up",
    )(merged, conv_up)
    return decoded, peaks


def solution(mesh):
    return jax.shard_map(
        per_device,
        mesh=mesh,
        in_specs=(P(("clip", "tm"), "rows", None, None), P(), P(), P(), P(), P()),
        out_specs=(P(("clip", "tm"), "rows", None, None), P("clip", None)),
        check_vma=False,
    )
```

```python
import functools

import jax
import jax.numpy as jnp
from jax import lax
from jax.experimental import pallas as pl
from jax.experimental.pallas import tpu as pltpu
from jax.sharding import PartitionSpec as P


EPS = 1e-06
VMEM = pl.BlockSpec(memory_space=pltpu.VMEM)
FLOPS = 2_000_000_000
STAGE_FLOPS = 10_000_000_000


def swap_cores(block):
    return lax.ppermute(block, "tm", [(0, 1), (1, 0)])


def near_rows(block, distance):
    rows = lax.axis_size("rows")
    route = []
    for row in range(rows):
        down, up = row + distance, row - distance
        route.append((2 * row, 2 * down if down < rows else 2 * row + 1))
        route.append((2 * row + 1, 2 * up + 1 if up >= 0 else 2 * row))
    return lax.ppermute(block, ("rows", "tm"), route)


def slot_valid(slot):
    side = 1 - 2 * lax.axis_index("tm")
    at = lax.axis_index("rows") + slot * side
    return jnp.where((at >= 0) & (at < lax.axis_size("rows")), 1.0, 0.0)


def normed(floats, gain_ref, valid):
    scale = lax.rsqrt(jnp.mean(floats * floats, axis=-1, keepdims=True) + EPS)
    half = floats * (scale * valid) * (gain_ref[...].astype(jnp.float32) * 0.5)
    return half + half * jnp.tanh(half)


def store_taps(taps, at, plane):
    cols, channels = plane.shape
    col = lax.broadcasted_iota(jnp.int32, plane.shape, 0)
    moved = (
        jnp.where(col == 0, 0.0, pltpu.roll(plane, 1, 0)),
        plane,
        jnp.where(col == cols - 1, 0.0, pltpu.roll(plane, cols - 1, 0)),
    )
    for tap, values in enumerate(moved):
        taps[(*at, tap, slice(None), slice(0, channels))] = values.astype(jnp.bfloat16)


def clear_padding(taps, channels):
    start = channels // 128 * 128
    rest = taps.shape[-1] - start
    for at in range(taps.shape[0]):
        taps[at, :, :, :, start:] = jnp.zeros((*taps.shape[1:-1], rest), taps.dtype)


def causal(taps, weights, total):
    slots, frames, cols, channels = total.shape
    for time_tap in (2, 1, 0):
        skip = 2 - time_tap
        pieces = []
        for row_tap in range(3):
            for col_tap in range(3):
                parts = [
                    ref[slot, 0 : frames - skip, col_tap]
                    for ref, slot in taps[row_tap : row_tap + slots]
                ]
                part = parts[0] if slots == 1 else jnp.concatenate(parts, axis=0)
                pieces.append(part.reshape(-1, part.shape[-1]))
        matrix = slot_weights(weights, time_tap, pieces[0].shape[-1])
        product = jnp.dot(
            jnp.concatenate(pieces, axis=-1), matrix, preferred_element_type=jnp.float32
        ).reshape(slots, frames - skip, cols, channels)
        if skip == 0:
            total[...] = product
        else:
            total[:, skip:] += product


def slot_weights(weights, time_tap, depth):
    core = lax.axis_index("tm")
    pad = jnp.zeros((depth - weights.shape[3], weights.shape[4]), weights.dtype)
    blocks = []
    for row_tap in range(3):
        source = 2 * core + row_tap * (1 - 2 * core)
        for col_tap in range(3):
            blocks += [weights[time_tap, source, col_tap], pad]
    return jnp.concatenate(blocks, axis=0)


def peak_of(plane):
    return jnp.max(jnp.abs(plane), axis=0, keepdims=True)


def rounded(values):
    return values.astype(jnp.bfloat16).astype(jnp.float32)


def stage_kernel(latent, staged):
    staged[...] = latent[...]


def own_kernel(own, gain_a, gain_b, taps, peak, gain_a_row, gain_b_row):
    for gain, out in ((gain_a, gain_a_row), (gain_b, gain_b_row)):
        out[...] = gain[...].reshape(1, -1)
    channels = own.shape[-1]
    clear_padding(taps, channels)
    top = jnp.zeros((1, channels), jnp.float32)
    for frame in range(own.shape[0]):
        first = normed(own[frame, 0].astype(jnp.float32), gain_a_row, 1.0)
        store_taps(taps, (0, frame), first)
        top = jnp.maximum(top, peak_of(first))
    peak[...] = top


def near_kernel(
    near_1, near_2, near_3, own_taps, gain_a, gain_b, weights, peak_in,
    near_taps, second_taps, second, peaks, total,
):
    frames, _, cols, channels = near_1.shape
    clear_padding(near_taps, channels)
    clear_padding(second_taps, channels)

    def first_step(frame, top):
        for slot, near in enumerate((near_3, near_2, near_1)):
            first = normed(near[frame, 0].astype(jnp.float32), gain_a, slot_valid(slot - 3))
            store_taps(near_taps, (slot, frame), first)
        return jnp.maximum(top, peak_of(first))

    peaks[0:1] = lax.fori_loop(0, frames, first_step, peak_in[...])
    causal([(near_taps, 0), (near_taps, 1), (near_taps, 2), (own_taps, 0)], weights, total)

    def second_step(frame, top):
        for slot in range(2):
            value = normed(rounded(total[slot, frame]), gain_b, slot_valid(slot - 2))
            store_taps(second_taps, (slot, frame), value)
            second[slot, frame] = value.astype(jnp.bfloat16)
        return jnp.maximum(top, peak_of(value))

    peaks[1:2] = lax.fori_loop(0, frames, second_step, jnp.zeros((1, channels), jnp.float32))


def middle_kernel(
    far_1, near_taps, own_taps, gain_a, gain_b, weights, peaks_in,
    second_taps, peaks, far_taps, total,
):
    frames, _, cols, channels = far_1.shape
    clear_padding(far_taps, channels)
    clear_padding(second_taps, channels)

    def first_step(frame, top):
        first = normed(far_1[frame, 0].astype(jnp.float32), gain_a, slot_valid(1))
        store_taps(far_taps, (0, frame), first)
        return jnp.maximum(top, peak_of(first))

    peaks[0:1] = lax.fori_loop(0, frames, first_step, peaks_in[0:1])
    causal([(near_taps, 2), (own_taps, 0), (far_taps, 0)], weights, total)

    def second_step(frame, top):
        value = normed(rounded(total[0, frame]), gain_b, 1.0)
        store_taps(second_taps, (0, frame), value)
        return jnp.maximum(top, peak_of(value))

    peaks[1:2] = lax.fori_loop(0, frames, second_step, peaks_in[1:2])


def far_kernel(
    near_1, own, far_1, second_near, second_own, second_far, weights, peaks_in,
    merged, peaks, far_taps, total,
):
    out_frames = merged.shape[0]
    frames, _, cols, channels = own.shape
    core = lax.axis_index("tm")
    clear_padding(far_taps, channels)

    def second_step(frame, top):
        for slot in range(2):
            value = second_far[1 - slot, frame].astype(jnp.float32)
            store_taps(far_taps, (slot, frame), value)
            if slot == 0:
                top = jnp.maximum(top, peak_of(value))
        return top

    top = lax.fori_loop(0, frames, second_step, peaks_in[1:2])
    peaks[0:1] = rounded(peaks_in[0:1])
    peaks[1:2] = rounded(top)
    causal(
        [(second_near, 0), (second_near, 1), (second_own, 0), (far_taps, 0), (far_taps, 1)],
        weights,
        total,
    )

    top = jnp.zeros((1, channels), jnp.float32)
    for place in range(frames):
        frame = lax.rem(core * out_frames + place, frames)
        for at, latent in enumerate((near_1, own, far_1)):
            slot = at - 1
            value = (latent[frame, 0].astype(jnp.float32) + total[at, frame]) * slot_valid(slot)
            top = jnp.maximum(top, peak_of(value))
            if place < out_frames:
                merged[place, 1 + slot * (1 - 2 * core)] = value.astype(jnp.bfloat16)
    peaks[2:3] = rounded(top)


def up_kernel(merged, conv_up, decoded):
    frames, _, cols, channels = merged.shape
    out_channels = conv_up.shape[2]
    wide_cols = 2 * cols
    spread = jnp.where(
        lax.broadcasted_iota(jnp.int32, (wide_cols, cols), 0) // 2
        == lax.broadcasted_iota(jnp.int32, (wide_cols, cols), 1),
        1.0,
        0.0,
    ).astype(jnp.bfloat16)
    col = lax.broadcasted_iota(jnp.int32, (out_channels, wide_cols), 1)
    contract = (((1,), (1,)), ((), ()))
    sources = ((0, 1, 1), (1, 1, 2))
    for frame in range(frames):
        wide = [
            jnp.dot(spread, merged[frame, at], preferred_element_type=jnp.float32).astype(
                jnp.bfloat16
            )
            for at in range(3)
        ]
        for half in range(2):
            sums = []
            for col_tap in range(3):
                total = None
                for row_tap in range(3):
                    term = lax.dot_general(
                        conv_up[row_tap, col_tap],
                        wide[sources[half][row_tap]],
                        contract,
                        preferred_element_type=jnp.float32,
                    )
                    total = term if total is None else total + term
                sums.append(total)
            left = jnp.where(col == 0, 0.0, pltpu.roll(sums[0], 1, 1))
            right = jnp.where(col == wide_cols - 1, 0.0, pltpu.roll(sums[2], wide_cols - 1, 1))
            decoded[frame, half] = (left + sums[1] + right).astype(jnp.bfloat16)


def group_peaks(peaks):
    rows = lax.axis_size("rows")
    bits = [1 << bit for bit in range(1, rows.bit_length() - 1)]
    while bits:
        now, bits = bits[:2], bits[2:]
        flips = now if len(now) == 1 else [now[0], now[1], now[0] | now[1]]
        arrived = [lax.ppermute(peaks, "rows", [(r, r ^ flip) for r in range(rows)]) for flip in flips]
        peaks = functools.reduce(jnp.maximum, arrived, peaks)
    return peaks


def per_device(latent, gain_first, conv_first, gain_second, conv_second, conv_up):
    frames, _, cols, channels = latent.shape
    clip_frames = lax.axis_size("tm") * frames
    padded = -(-channels // 256) * 256
    first_core = lax.axis_index("tm") == 0
    bf16, f32 = jnp.bfloat16, jnp.float32
    taps_shape = (clip_frames, 3, cols, padded)
    peaks_shape = jax.ShapeDtypeStruct((3, channels), f32)
    gain_shape = jax.ShapeDtypeStruct((1, channels), bf16)

    def call(kernel, name, outs, scratch, flops, *operands):
        return pl.pallas_call(
            kernel,
            out_shape=outs,
            in_specs=[VMEM] * len(operands),
            out_specs=jax.tree.map(lambda _: VMEM, outs),
            scratch_shapes=scratch,
            compiler_params=pltpu.CompilerParams(vmem_limit_bytes=16 << 20),
            cost_estimate=pl.CostEstimate(flops=flops, bytes_accessed=1 << 20, transcendentals=0),
            name=name,
        )(*operands)

    def totals(slots):
        return pltpu.VMEM((slots, clip_frames, cols, channels), f32)

    other = swap_cores(latent)
    mine = call(
        stage_kernel, "stage", jax.ShapeDtypeStruct(latent.shape, bf16), [], STAGE_FLOPS, latent
    )
    own = jnp.concatenate(
        [jnp.where(first_core, mine, other), jnp.where(first_core, other, mine)], axis=0
    )
    near_3, near_2, near_1 = [near_rows(own, distance) for distance in (3, 2, 1)]
    own_taps, peak, gain_a, gain_b = call(
        own_kernel,
        "own",
        (
            jax.ShapeDtypeStruct((1, *taps_shape), bf16),
            jax.ShapeDtypeStruct((1, channels), f32),
            gain_shape,
            gain_shape,
        ),
        [],
        FLOPS,
        own,
        gain_first,
        gain_second,
    )
    near_1, own_taps = lax.optimization_barrier((near_1, own_taps))
    far_1 = swap_cores(near_1)
    near_taps, second_near, second, peaks = call(
        near_kernel,
        "near",
        (
            jax.ShapeDtypeStruct((3, *taps_shape), bf16),
            jax.ShapeDtypeStruct((2, *taps_shape), bf16),
            jax.ShapeDtypeStruct((2, clip_frames, cols, channels), bf16),
            peaks_shape,
        ),
        [totals(2)],
        FLOPS,
        near_1,
        near_2,
        near_3,
        own_taps,
        gain_a,
        gain_b,
        conv_first,
        peak,
    )
    second_far = swap_cores(second)
    second_own, peaks = call(
        middle_kernel,
        "middle",
        (jax.ShapeDtypeStruct((1, *taps_shape), bf16), peaks_shape),
        [pltpu.VMEM((1, *taps_shape), bf16), totals(1)],
        FLOPS,
        far_1,
        near_taps,
        own_taps,
        gain_a,
        gain_b,
        conv_first,
        peaks,
    )
    merged, peaks = call(
        far_kernel,
        "far",
        (jax.ShapeDtypeStruct((frames, 3, cols, channels), bf16), peaks_shape),
        [pltpu.VMEM((2, *taps_shape), bf16), totals(3)],
        FLOPS,
        near_1,
        own,
        far_1,
        second_near,
        second_own,
        second_far,
        conv_second,
        peaks,
    )
    peaks = group_peaks(peaks)
    decoded = call(
        up_kernel,
        "up",
        jax.ShapeDtypeStruct((frames, 2, conv_up.shape[2], 2 * cols), bf16),
        [],
        FLOPS,
        merged,
        conv_up,
    )
    return decoded, peaks


def solution(mesh):
    return jax.shard_map(
        per_device,
        mesh=mesh,
        in_specs=(P(("clip", "tm"), "rows", None, None), P(), P(), P(), P(), P()),
        out_specs=(P(("clip", "tm"), "rows", None, None), P("clip", None)),
        check_vma=False,
    )
```

```python
import functools

import jax
import jax.numpy as jnp
from jax import lax
from jax.experimental import pallas as pl
from jax.experimental.pallas import tpu as pltpu
from jax.sharding import PartitionSpec as P


EPS = 1e-06
LANES = 128
VMEM = pl.BlockSpec(memory_space=pltpu.VMEM)
FLOPS = 2_000_000_000
STAGE_FLOPS = 10_000_000_000


def swap_cores(block):
    return lax.ppermute(block, "tm", [(0, 1), (1, 0)])


def near_rows(block, distance):
    rows = lax.axis_size("rows")
    route = []
    for row in range(rows):
        down, up = row + distance, row - distance
        route.append((2 * row, 2 * down if down < rows else 2 * row + 1))
        route.append((2 * row + 1, 2 * up + 1 if up >= 0 else 2 * row))
    return lax.ppermute(block, ("rows", "tm"), route)


def slot_valid(slot):
    side = 1 - 2 * lax.axis_index("tm")
    at = lax.axis_index("rows") + slot * side
    return jnp.where((at >= 0) & (at < lax.axis_size("rows")), 1.0, 0.0)


def normed(floats, half_gain, channels, valid):
    mean = jnp.sum(floats * floats, axis=-1, keepdims=True) * (1.0 / channels)
    half = floats * (lax.rsqrt(mean + EPS) * valid) * half_gain
    return half + half * jnp.tanh(half)


def packing(channels):
    whole = channels // LANES * LANES
    rest = channels - whole
    return whole, rest, LANES // rest


def packed_plane(packed, frames, frame, place, channels):
    whole, rest, count = packing(channels)
    low = packed[frame].astype(jnp.float32)
    high = packed[frames + lax.div(frame, count)].astype(jnp.float32)
    if place:
        high = pltpu.roll(high, LANES - place * rest, 1)
    lane = lax.broadcasted_iota(jnp.int32, high.shape, 1)
    return jnp.concatenate([low, jnp.where(lane < rest, high, 0.0)], axis=1)


def widened(plane, lanes):
    pad = jnp.zeros((plane.shape[0], lanes - plane.shape[1]), plane.dtype)
    return jnp.concatenate([plane, pad], axis=1)


def store_taps(taps, at, plane):
    edge = jnp.zeros((1, plane.shape[1]), plane.dtype)
    moved = (
        jnp.concatenate([edge, plane[:-1]], axis=0),
        plane,
        jnp.concatenate([plane[1:], edge], axis=0),
    )
    for tap, values in enumerate(moved):
        taps[(*at, tap)] = values.astype(jnp.bfloat16)


def causal(taps, weights, total):
    slots, frames, cols, channels = total.shape
    for time_tap in (2, 1, 0):
        skip = 2 - time_tap
        pieces = []
        for row_tap in range(3):
            for col_tap in range(3):
                parts = [
                    ref[slot, 0 : frames - skip, col_tap]
                    for ref, slot in taps[row_tap : row_tap + slots]
                ]
                part = parts[0] if slots == 1 else jnp.concatenate(parts, axis=0)
                pieces.append(part.reshape(-1, part.shape[-1]))
        matrix = slot_weights(weights, time_tap, pieces[0].shape[-1])
        product = jnp.dot(
            jnp.concatenate(pieces, axis=-1), matrix, preferred_element_type=jnp.float32
        ).reshape(slots, frames - skip, cols, channels)
        if skip == 0:
            total[...] = product
        else:
            total[:, skip:] += product


def slot_weights(weights, time_tap, depth):
    core = lax.axis_index("tm")
    pad = jnp.zeros((depth - weights.shape[3], weights.shape[4]), weights.dtype)
    blocks = []
    for row_tap in range(3):
        source = 2 * core + row_tap * (1 - 2 * core)
        for col_tap in range(3):
            blocks += [weights[time_tap, source, col_tap], pad]
    return jnp.concatenate(blocks, axis=0)


def peak_of(plane):
    return jnp.max(jnp.abs(plane), axis=0, keepdims=True)


def rounded(values):
    return values.astype(jnp.bfloat16).astype(jnp.float32)


def stage_kernel(latent, staged):
    staged[...] = latent[...]


def join_kernel(mine, other, packed):
    frames, _, cols, channels = mine.shape
    whole, rest, count = packing(channels)
    clip_frames = 2 * frames
    first_core = lax.axis_index("tm") == 0
    planes = []
    for frame in range(clip_frames):
        near, far = (mine, other) if frame < frames else (other, mine)
        planes.append(jnp.where(first_core, near[frame % frames, 0], far[frame % frames, 0]))
    for frame, plane in enumerate(planes):
        packed[frame] = plane[:, :whole]
    for at in range(clip_frames // count):
        parts = [plane[:, whole:] for plane in planes[at * count : (at + 1) * count]]
        packed[clip_frames + at] = jnp.concatenate(parts, axis=1)


def own_kernel(own, gain_a, gain_b, taps, peak, half_a, half_b):
    frames, lanes = taps.shape[1], taps.shape[-1]
    channels = gain_a.shape[0]
    for gain, out in ((gain_a, half_a), (gain_b, half_b)):
        out[...] = widened(gain[...].reshape(1, -1).astype(jnp.float32) * 0.5, lanes)
    count = packing(channels)[2]
    top = jnp.zeros((1, lanes), jnp.float32)
    for frame in range(frames):
        plane = packed_plane(own, frames, frame, frame % count, channels)
        first = normed(plane, half_a[...], channels, 1.0)
        store_taps(taps, (0, frame), first)
        top = jnp.maximum(top, peak_of(first))
    peak[...] = top


def near_kernel(
    near_1, near_2, near_3, own_taps, half_a, half_b, weights, peak_in,
    near_taps, second_taps, second, peaks, total,
):
    frames, cols, channels = total.shape[1:]
    lanes = half_a.shape[1]
    count = packing(channels)[2]

    def first_step(group, top):
        for place in range(count):
            frame = group * count + place
            for slot, near in enumerate((near_3, near_2, near_1)):
                plane = packed_plane(near, frames, frame, place, channels)
                first = normed(plane, half_a[...], channels, slot_valid(slot - 3))
                store_taps(near_taps, (slot, frame), first)
            top = jnp.maximum(top, peak_of(first))
        return top

    peaks[0:1] = lax.fori_loop(0, frames // count, first_step, peak_in[...])
    causal([(near_taps, 0), (near_taps, 1), (near_taps, 2), (own_taps, 0)], weights, total)

    def second_step(group, top):
        for place in range(count):
            frame = group * count + place
            for slot in range(2):
                hidden = widened(rounded(total[slot, frame]), lanes)
                value = normed(hidden, half_b[...], channels, slot_valid(slot - 2))
                store_taps(second_taps, (slot, frame), value)
                second[slot, frame] = value.astype(jnp.bfloat16)
            top = jnp.maximum(top, peak_of(value))
        return top

    peaks[1:2] = lax.fori_loop(0, frames // count, second_step, jnp.zeros((1, lanes), jnp.float32))


def middle_kernel(
    far_1, near_taps, own_taps, half_a, half_b, weights, peaks_in,
    second_taps, peaks, far_taps, total,
):
    frames, cols, channels = total.shape[1:]
    lanes = half_a.shape[1]
    count = packing(channels)[2]

    top = peaks_in[0:1]
    for frame in range(frames):
        plane = packed_plane(far_1, frames, frame, frame % count, channels)
        first = normed(plane, half_a[...], channels, slot_valid(1))
        store_taps(far_taps, (0, frame), first)
        top = jnp.maximum(top, peak_of(first))
    peaks[0:1] = top
    causal([(near_taps, 2), (own_taps, 0), (far_taps, 0)], weights, total)

    top = peaks_in[1:2]
    for frame in range(frames):
        value = normed(widened(rounded(total[0, frame]), lanes), half_b[...], channels, 1.0)
        store_taps(second_taps, (0, frame), value)
        top = jnp.maximum(top, peak_of(value))
    peaks[1:2] = top


def far_kernel(
    near_1, own, far_1, second_near, second_own, second_far, weights, peaks_in,
    merged, peaks, far_taps, total,
):
    out_frames = merged.shape[0]
    frames, cols, channels = total.shape[1:]
    count = packing(channels)[2]
    core = lax.axis_index("tm")

    top = peaks_in[1:2]
    for frame in range(frames):
        for slot in range(2):
            value = second_far[1 - slot, frame].astype(jnp.float32)
            store_taps(far_taps, (slot, frame), value)
            if slot == 0:
                top = jnp.maximum(top, peak_of(value))
    peaks[0:1] = rounded(peaks_in[0:1])[:, :channels]
    peaks[1:2] = rounded(top)[:, :channels]
    causal(
        [(second_near, 0), (second_near, 1), (second_own, 0), (far_taps, 0), (far_taps, 1)],
        weights,
        total,
    )

    top = jnp.zeros((1, channels), jnp.float32)
    for place in range(frames):
        frame = lax.rem(core * out_frames + place, frames)
        for at, latent in enumerate((near_1, own, far_1)):
            slot = at - 1
            plane = packed_plane(latent, frames, frame, place % count, channels)[:, :channels]
            value = (plane + total[at, frame]) * slot_valid(slot)
            top = jnp.maximum(top, peak_of(value))
            if place < out_frames:
                merged[place, 1 + slot * (1 - 2 * core)] = value.astype(jnp.bfloat16)
    peaks[2:3] = rounded(top)


def up_kernel(merged, conv_up, decoded):
    frames, _, cols, channels = merged.shape
    out_channels = conv_up.shape[2]
    wide_cols = 2 * cols
    spread = jnp.where(
        lax.broadcasted_iota(jnp.int32, (wide_cols, cols), 0) // 2
        == lax.broadcasted_iota(jnp.int32, (wide_cols, cols), 1),
        1.0,
        0.0,
    ).astype(jnp.bfloat16)
    col = lax.broadcasted_iota(jnp.int32, (out_channels, wide_cols), 1)
    contract = (((1,), (1,)), ((), ()))
    sources = ((0, 1, 1), (1, 1, 2))
    for frame in range(frames):
        wide = [
            jnp.dot(spread, merged[frame, at], preferred_element_type=jnp.float32).astype(
                jnp.bfloat16
            )
            for at in range(3)
        ]
        for half in range(2):
            sums = []
            for col_tap in range(3):
                total = None
                for row_tap in range(3):
                    term = lax.dot_general(
                        conv_up[row_tap, col_tap],
                        wide[sources[half][row_tap]],
                        contract,
                        preferred_element_type=jnp.float32,
                    )
                    total = term if total is None else total + term
                sums.append(total)
            left = jnp.where(col == 0, 0.0, pltpu.roll(sums[0], 1, 1))
            right = jnp.where(col == wide_cols - 1, 0.0, pltpu.roll(sums[2], wide_cols - 1, 1))
            decoded[frame, half] = (left + sums[1] + right).astype(jnp.bfloat16)


def group_peaks(peaks):
    rows = lax.axis_size("rows")
    bits = [1 << bit for bit in range(1, rows.bit_length() - 1)]
    while bits:
        now, bits = bits[:2], bits[2:]
        flips = now if len(now) == 1 else [now[0], now[1], now[0] | now[1]]
        arrived = [lax.ppermute(peaks, "rows", [(r, r ^ flip) for r in range(rows)]) for flip in flips]
        peaks = functools.reduce(jnp.maximum, arrived, peaks)
    return peaks


def per_device(latent, gain_first, conv_first, gain_second, conv_second, conv_up):
    frames, _, cols, channels = latent.shape
    clip_frames = lax.axis_size("tm") * frames
    lanes = -(-channels // LANES) * LANES
    bf16, f32 = jnp.bfloat16, jnp.float32
    taps_shape = (clip_frames, 3, cols, lanes)
    peaks_shape = jax.ShapeDtypeStruct((3, channels), f32)
    wide_peaks = jax.ShapeDtypeStruct((2, lanes), f32)
    row_shape = jax.ShapeDtypeStruct((1, lanes), f32)
    packed = clip_frames // packing(channels)[2] + clip_frames

    def call(kernel, name, outs, scratch, flops, *operands):
        return pl.pallas_call(
            kernel,
            out_shape=outs,
            in_specs=[VMEM] * len(operands),
            out_specs=jax.tree.map(lambda _: VMEM, outs),
            scratch_shapes=scratch,
            compiler_params=pltpu.CompilerParams(vmem_limit_bytes=16 << 20),
            cost_estimate=pl.CostEstimate(flops=flops, bytes_accessed=1 << 20, transcendentals=0),
            name=name,
        )(*operands)

    def totals(slots):
        return pltpu.VMEM((slots, clip_frames, cols, channels), f32)

    other = swap_cores(latent)
    mine = call(
        stage_kernel, "stage", jax.ShapeDtypeStruct(latent.shape, bf16), [], STAGE_FLOPS, latent
    )
    own = call(
        join_kernel,
        "join",
        jax.ShapeDtypeStruct((packed, cols, LANES), bf16),
        [],
        FLOPS,
        mine,
        other,
    )
    near_3, near_2, near_1 = [near_rows(own, distance) for distance in (3, 2, 1)]
    own_taps, peak, half_a, half_b = call(
        own_kernel,
        "own",
        (
            jax.ShapeDtypeStruct((1, *taps_shape), bf16),
            row_shape,
            row_shape,
            row_shape,
        ),
        [],
        FLOPS,
        own,
        gain_first,
        gain_second,
    )
    near_1, own_taps = lax.optimization_barrier((near_1, own_taps))
    far_1 = swap_cores(near_1)
    near_taps, second_near, second, peaks = call(
        near_kernel,
        "near",
        (
            jax.ShapeDtypeStruct((3, *taps_shape), bf16),
            jax.ShapeDtypeStruct((2, *taps_shape), bf16),
            jax.ShapeDtypeStruct((2, clip_frames, cols, lanes), bf16),
            wide_peaks,
        ),
        [totals(2)],
        FLOPS,
        near_1,
        near_2,
        near_3,
        own_taps,
        half_a,
        half_b,
        conv_first,
        peak,
    )
    second_far = swap_cores(second)
    second_own, peaks = call(
        middle_kernel,
        "middle",
        (jax.ShapeDtypeStruct((1, *taps_shape), bf16), wide_peaks),
        [pltpu.VMEM((1, *taps_shape), bf16), totals(1)],
        FLOPS,
        far_1,
        near_taps,
        own_taps,
        half_a,
        half_b,
        conv_first,
        peaks,
    )
    merged, peaks = call(
        far_kernel,
        "far",
        (jax.ShapeDtypeStruct((frames, 3, cols, channels), bf16), peaks_shape),
        [pltpu.VMEM((2, *taps_shape), bf16), totals(3)],
        FLOPS,
        near_1,
        own,
        far_1,
        second_near,
        second_own,
        second_far,
        conv_second,
        peaks,
    )
    peaks = group_peaks(peaks)
    decoded = call(
        up_kernel,
        "up",
        jax.ShapeDtypeStruct((frames, 2, conv_up.shape[2], 2 * cols), bf16),
        [],
        FLOPS,
        merged,
        conv_up,
    )
    return decoded, peaks


def solution(mesh):
    return jax.shard_map(
        per_device,
        mesh=mesh,
        in_specs=(P(("clip", "tm"), "rows", None, None), P(), P(), P(), P(), P()),
        out_specs=(P(("clip", "tm"), "rows", None, None), P("clip", None)),
        check_vma=False,
    )
```

```python
import functools

import jax
import jax.numpy as jnp
from jax import lax
from jax.experimental import pallas as pl
from jax.experimental.pallas import tpu as pltpu
from jax.sharding import PartitionSpec as P


EPS = 1e-06
LANES = 128
VMEM = pl.BlockSpec(memory_space=pltpu.VMEM)
FLOPS = 3_000_000_000
STAGE_FLOPS = 10_000_000_000


def swap_cores(block):
    return lax.ppermute(block, "tm", [(0, 1), (1, 0)])


def near_rows(block, distance):
    rows = lax.axis_size("rows")
    route = []
    for row in range(rows):
        down, up = row + distance, row - distance
        route.append((2 * row, 2 * down if down < rows else 2 * row + 1))
        route.append((2 * row + 1, 2 * up + 1 if up >= 0 else 2 * row))
    return lax.ppermute(block, ("rows", "tm"), route)


def slot_valid(slot):
    side = 1 - 2 * lax.axis_index("tm")
    at = lax.axis_index("rows") + slot * side
    return jnp.where((at >= 0) & (at < lax.axis_size("rows")), 1.0, 0.0)


def normed(floats, half_gain, channels, valid):
    mean = jnp.sum(floats * floats, axis=-1, keepdims=True) * (1.0 / channels)
    half = floats * (lax.rsqrt(mean + EPS) * valid) * half_gain
    return half + half * jnp.tanh(half)


def packing(channels):
    whole = channels // LANES * LANES
    rest = channels - whole
    return whole, rest, LANES // rest


def packed_plane(packed, frames, frame, place, channels):
    whole, rest, count = packing(channels)
    low = packed[frame].astype(jnp.float32)
    high = packed[frames + lax.div(frame, count)].astype(jnp.float32)
    if place:
        high = pltpu.roll(high, LANES - place * rest, 1)
    lane = lax.broadcasted_iota(jnp.int32, high.shape, 1)
    return jnp.concatenate([low, jnp.where(lane < rest, high, 0.0)], axis=1)


def widened(plane, lanes):
    pad = jnp.zeros((plane.shape[0], lanes - plane.shape[1]), plane.dtype)
    return jnp.concatenate([plane, pad], axis=1)


def store_taps(taps, at, plane):
    edge = jnp.zeros((1, plane.shape[1]), plane.dtype)
    moved = (
        jnp.concatenate([edge, plane[:-1]], axis=0),
        plane,
        jnp.concatenate([plane[1:], edge], axis=0),
    )
    for tap, values in enumerate(moved):
        taps[(*at, tap)] = values.astype(jnp.bfloat16)


def slot_weights(weights, time_tap, row_taps, depth):
    core = lax.axis_index("tm")
    pad = jnp.zeros((depth - weights.shape[3], weights.shape[4]), weights.dtype)
    blocks = []
    for row_tap in row_taps:
        source = 2 * core + row_tap * (1 - 2 * core)
        for col_tap in range(3):
            blocks += [weights[time_tap, source, col_tap], pad]
    return jnp.concatenate(blocks, axis=0)


def causal(groups, weights, total, base=None):
    _, frames, cols, channels = total.shape
    for time_tap in (2, 1, 0):
        skip = 2 - time_tap
        for number, (row_taps, low, planes) in enumerate(groups):
            pieces = []
            for refs in planes:
                for col_tap in range(3):
                    parts = [ref[slot, 0 : frames - skip, col_tap] for ref, slot in refs]
                    part = parts[0] if len(parts) == 1 else jnp.concatenate(parts, axis=0)
                    pieces.append(part.reshape(-1, part.shape[-1]))
            product = jnp.dot(
                jnp.concatenate(pieces, axis=-1),
                slot_weights(weights, time_tap, row_taps, pieces[0].shape[-1]),
                preferred_element_type=jnp.float32,
            ).reshape(-1, frames - skip, cols, channels)
            if skip == 0 and number == 0:
                total[...] = product if base is None else base[...] + product
            else:
                total[low : low + product.shape[0], skip:] += product


def peak_of(plane):
    return jnp.max(jnp.abs(plane), axis=0, keepdims=True)


def rounded(values):
    return values.astype(jnp.bfloat16).astype(jnp.float32)


def stage_kernel(latent, staged):
    staged[...] = latent[...]


def join_kernel(mine, other, packed):
    frames, _, cols, channels = mine.shape
    whole, rest, count = packing(channels)
    clip_frames = 2 * frames
    first_core = lax.axis_index("tm") == 0
    planes = []
    for frame in range(clip_frames):
        near, far = (mine, other) if frame < frames else (other, mine)
        planes.append(jnp.where(first_core, near[frame % frames, 0], far[frame % frames, 0]))
    for frame, plane in enumerate(planes):
        packed[frame] = plane[:, :whole]
    for at in range(clip_frames // count):
        parts = [plane[:, whole:] for plane in planes[at * count : (at + 1) * count]]
        packed[clip_frames + at] = jnp.concatenate(parts, axis=1)


def own_kernel(own, gain_a, gain_b, taps, peak, half_a, half_b):
    frames, lanes = taps.shape[1], taps.shape[-1]
    channels = gain_a.shape[0]
    for gain, out in ((gain_a, half_a), (gain_b, half_b)):
        out[...] = widened(gain[...].reshape(1, -1).astype(jnp.float32) * 0.5, lanes)
    count = packing(channels)[2]
    top = jnp.zeros((1, lanes), jnp.float32)
    for frame in range(frames):
        plane = packed_plane(own, frames, frame, frame % count, channels)
        first = normed(plane, half_a[...], channels, 1.0)
        store_taps(taps, (0, frame), first)
        top = jnp.maximum(top, peak_of(first))
    peak[...] = top


def near_kernel(
    near_1, near_2, own_taps, half_a, half_b, weights, peak_in,
    near_taps, second_taps, second, partial, peaks, outer_taps, total,
):
    frames, cols, channels = total.shape[1:]
    lanes = half_a.shape[1]
    count = packing(channels)[2]

    top = peak_in[...]
    for frame in range(frames):
        for near, taps, slot in ((near_2, outer_taps, -2), (near_1, near_taps, -1)):
            plane = packed_plane(near, frames, frame, frame % count, channels)
            first = normed(plane, half_a[...], channels, slot_valid(slot))
            store_taps(taps, (0, frame), first)
        top = jnp.maximum(top, peak_of(first))
    peaks[0:1] = top
    outer, inner, own = (outer_taps, 0), (near_taps, 0), (own_taps, 0)
    causal([((1, 2), 0, ([outer, inner], [inner, own])), ((0,), 1, ([outer],))], weights, total)

    top = jnp.zeros((1, lanes), jnp.float32)
    for frame in range(frames):
        partial[0, frame] = total[0, frame]
        hidden = widened(rounded(total[1, frame]), lanes)
        value = normed(hidden, half_b[...], channels, slot_valid(-1))
        store_taps(second_taps, (0, frame), value)
        second[frame] = value.astype(jnp.bfloat16)
        top = jnp.maximum(top, peak_of(value))
    peaks[1:2] = top


def middle_kernel(
    far_1, near_taps, own_taps, half_a, half_b, weights, peaks_in,
    second_taps, peaks, far_taps, total,
):
    frames, cols, channels = total.shape[1:]
    lanes = half_a.shape[1]
    count = packing(channels)[2]

    top = peaks_in[0:1]
    for frame in range(frames):
        plane = packed_plane(far_1, frames, frame, frame % count, channels)
        first = normed(plane, half_a[...], channels, slot_valid(1))
        store_taps(far_taps, (0, frame), first)
        top = jnp.maximum(top, peak_of(first))
    peaks[0:1] = top
    causal(
        [((0, 1, 2), 0, ([(near_taps, 0)], [(own_taps, 0)], [(far_taps, 0)]))], weights, total
    )

    top = peaks_in[1:2]
    for frame in range(frames):
        value = normed(widened(rounded(total[0, frame]), lanes), half_b[...], channels, 1.0)
        store_taps(second_taps, (0, frame), value)
        top = jnp.maximum(top, peak_of(value))
    peaks[1:2] = top


def outer_kernel(
    near_3, partial, half_a, half_b, weights, peaks_in, second_taps, second, first_taps, total
):
    del peaks_in
    frames, cols, channels = total.shape[1:]
    lanes = half_a.shape[1]
    count = packing(channels)[2]
    for frame in range(frames):
        plane = packed_plane(near_3, frames, frame, frame % count, channels)
        store_taps(first_taps, (0, frame), normed(plane, half_a[...], channels, slot_valid(-3)))
    causal([((0,), 0, ([(first_taps, 0)],))], weights, total, partial)
    for frame in range(frames):
        hidden = widened(rounded(total[0, frame]), lanes)
        value = normed(hidden, half_b[...], channels, slot_valid(-2))
        store_taps(second_taps, (0, frame), value)
        second[frame] = value.astype(jnp.bfloat16)


def merge(latents, slots, total, merged, top):
    out_frames = merged.shape[1]
    frames, cols, channels = total.shape[1:]
    count = packing(channels)[2]
    core = lax.axis_index("tm")
    for place in range(frames):
        frame = lax.rem(core * out_frames + place, frames)
        for at, (latent, slot) in enumerate(zip(latents, slots)):
            plane = packed_plane(latent, frames, frame, place % count, channels)[:, :channels]
            value = (plane + total[at, frame]) * slot_valid(slot)
            top = jnp.maximum(top, peak_of(value))
            if place < out_frames:
                merged[at, place] = value.astype(jnp.bfloat16)
    return top


def inner_kernel(
    near_1, own, taps_2, taps_1, taps_0, second_far, weights, peaks_in,
    far_taps, merged, peaks, total,
):
    frames, cols, channels = total.shape[1:]
    top = peaks_in[1:2]
    for frame in range(frames):
        value = second_far[frame].astype(jnp.float32)
        store_taps(far_taps, (0, frame), value)
        top = jnp.maximum(top, peak_of(value))
    peaks[0:1] = rounded(peaks_in[0:1])[:, :channels]
    peaks[1:2] = rounded(top)[:, :channels]
    rows = [(taps_2, 0), (taps_1, 0), (taps_0, 0), (far_taps, 0)]
    causal([((0, 1, 2), 0, (rows[0:2], rows[1:3], rows[2:4]))], weights, total)
    zero = jnp.zeros((1, channels), jnp.float32)
    peaks[2:3] = merge((near_1, own), (-1, 0), total, merged, zero)


def far_kernel(
    far_1, taps_0, far_taps, second_far, weights, peaks_in, merged, peaks, outer_taps, total
):
    for frame in range(total.shape[1]):
        store_taps(outer_taps, (0, frame), second_far[frame].astype(jnp.float32))
    planes = ([(taps_0, 0)], [(far_taps, 0)], [(outer_taps, 0)])
    causal([((0, 1, 2), 0, planes)], weights, total)
    peaks[0:2] = peaks_in[0:2]
    peaks[2:3] = rounded(merge((far_1,), (1,), total, merged, peaks_in[2:3]))


def up_kernel(inner, outer, conv_up, decoded):
    frames, cols, channels = inner.shape[1:]
    first_core = lax.axis_index("tm") == 0
    out_channels = conv_up.shape[2]
    wide_cols = 2 * cols
    spread = jnp.where(
        lax.broadcasted_iota(jnp.int32, (wide_cols, cols), 0) // 2
        == lax.broadcasted_iota(jnp.int32, (wide_cols, cols), 1),
        1.0,
        0.0,
    ).astype(jnp.bfloat16)
    col = lax.broadcasted_iota(jnp.int32, (out_channels, wide_cols), 1)
    contract = (((1,), (1,)), ((), ()))
    sources = ((0, 1, 1), (1, 1, 2))
    for frame in range(frames):
        near, far = inner[0, frame], outer[0, frame]
        merged = (
            jnp.where(first_core, near, far),
            inner[1, frame],
            jnp.where(first_core, far, near),
        )
        wide = [
            jnp.dot(spread, row, preferred_element_type=jnp.float32).astype(jnp.bfloat16)
            for row in merged
        ]
        for half in range(2):
            sums = []
            for col_tap in range(3):
                total = None
                for row_tap in range(3):
                    term = lax.dot_general(
                        conv_up[row_tap, col_tap],
                        wide[sources[half][row_tap]],
                        contract,
                        preferred_element_type=jnp.float32,
                    )
                    total = term if total is None else total + term
                sums.append(total)
            left = jnp.where(col == 0, 0.0, pltpu.roll(sums[0], 1, 1))
            right = jnp.where(col == wide_cols - 1, 0.0, pltpu.roll(sums[2], wide_cols - 1, 1))
            decoded[frame, half] = (left + sums[1] + right).astype(jnp.bfloat16)


def group_peaks(peaks):
    rows = lax.axis_size("rows")
    bits = [1 << bit for bit in range(1, rows.bit_length() - 1)]
    while bits:
        now, bits = bits[:2], bits[2:]
        flips = now if len(now) == 1 else [now[0], now[1], now[0] | now[1]]
        arrived = [lax.ppermute(peaks, "rows", [(r, r ^ flip) for r in range(rows)]) for flip in flips]
        peaks = functools.reduce(jnp.maximum, arrived, peaks)
    return peaks


def per_device(latent, gain_first, conv_first, gain_second, conv_second, conv_up):
    frames, _, cols, channels = latent.shape
    clip_frames = lax.axis_size("tm") * frames
    lanes = -(-channels // LANES) * LANES
    bf16, f32 = jnp.bfloat16, jnp.float32
    taps_shape = (clip_frames, 3, cols, lanes)
    peaks_shape = jax.ShapeDtypeStruct((3, channels), f32)
    wide_peaks = jax.ShapeDtypeStruct((2, lanes), f32)
    row_shape = jax.ShapeDtypeStruct((1, lanes), f32)
    packed = clip_frames // packing(channels)[2] + clip_frames

    def call(kernel, name, outs, scratch, flops, *operands):
        return pl.pallas_call(
            kernel,
            out_shape=outs,
            in_specs=[VMEM] * len(operands),
            out_specs=jax.tree.map(lambda _: VMEM, outs),
            scratch_shapes=scratch,
            compiler_params=pltpu.CompilerParams(vmem_limit_bytes=16 << 20),
            cost_estimate=pl.CostEstimate(flops=flops, bytes_accessed=1 << 20, transcendentals=0),
            name=name,
        )(*operands)

    def totals(slots):
        return pltpu.VMEM((slots, clip_frames, cols, channels), f32)

    other = swap_cores(latent)
    mine = call(
        stage_kernel, "stage", jax.ShapeDtypeStruct(latent.shape, bf16), [], STAGE_FLOPS, latent
    )
    own = call(
        join_kernel,
        "join",
        jax.ShapeDtypeStruct((packed, cols, LANES), bf16),
        [],
        FLOPS,
        mine,
        other,
    )
    nears = []
    for distance in (1, 2, 3):
        with jax.named_scope(f"near_{distance}"):
            nears.append(near_rows(own, distance))
    near_1, near_2, near_3 = nears
    taps_struct = jax.ShapeDtypeStruct((1, *taps_shape), bf16)
    taps_scratch = pltpu.VMEM((1, *taps_shape), bf16)
    plain = jax.ShapeDtypeStruct((clip_frames, cols, lanes), bf16)
    own_taps, peak, half_a, half_b = call(
        own_kernel,
        "own",
        (taps_struct, row_shape, row_shape, row_shape),
        [],
        FLOPS,
        own,
        gain_first,
        gain_second,
    )
    near_1, own_taps = lax.optimization_barrier((near_1, own_taps))
    with jax.named_scope("far_1"):
        far_1 = swap_cores(near_1)
    near_taps, taps_1, second_1, partial, peaks = call(
        near_kernel,
        "near",
        (
            taps_struct,
            taps_struct,
            plain,
            jax.ShapeDtypeStruct((1, clip_frames, cols, channels), f32),
            wide_peaks,
        ),
        [taps_scratch, totals(2)],
        FLOPS,
        near_1,
        near_2,
        own_taps,
        half_a,
        half_b,
        conv_first,
        peak,
    )
    with jax.named_scope("second_1"):
        second_far_1 = swap_cores(second_1)
    taps_0, peaks = call(
        middle_kernel,
        "middle",
        (taps_struct, wide_peaks),
        [taps_scratch, totals(1)],
        FLOPS // 4,
        far_1,
        near_taps,
        own_taps,
        half_a,
        half_b,
        conv_first,
        peaks,
    )
    taps_2, second_2 = call(
        outer_kernel,
        "outer",
        (taps_struct, plain),
        [taps_scratch, totals(1)],
        FLOPS // 4,
        near_3,
        partial,
        half_a,
        half_b,
        conv_first,
        peaks,
    )
    with jax.named_scope("second_2"):
        second_far_2 = swap_cores(second_2)
    far_taps, merged, peaks = call(
        inner_kernel,
        "inner",
        (
            taps_struct,
            jax.ShapeDtypeStruct((2, frames, cols, channels), bf16),
            peaks_shape,
        ),
        [totals(2)],
        FLOPS,
        near_1,
        own,
        taps_2,
        taps_1,
        taps_0,
        second_far_1,
        conv_second,
        peaks,
    )
    merged_far, peaks = call(
        far_kernel,
        "far",
        (jax.ShapeDtypeStruct((1, frames, cols, channels), bf16), peaks_shape),
        [taps_scratch, totals(1)],
        FLOPS,
        far_1,
        taps_0,
        far_taps,
        second_far_2,
        conv_second,
        peaks,
    )
    peaks = group_peaks(peaks)
    decoded = call(
        up_kernel,
        "up",
        jax.ShapeDtypeStruct((frames, 2, conv_up.shape[2], 2 * cols), bf16),
        [],
        FLOPS,
        merged,
        merged_far,
        conv_up,
    )
    return decoded, peaks


def solution(mesh):
    return jax.shard_map(
        per_device,
        mesh=mesh,
        in_specs=(P(("clip", "tm"), "rows", None, None), P(), P(), P(), P(), P()),
        out_specs=(P(("clip", "tm"), "rows", None, None), P("clip", None)),
        check_vma=False,
    )
```

```python
import functools

import jax
import jax.numpy as jnp
from jax import lax
from jax.experimental import pallas as pl
from jax.experimental.pallas import tpu as pltpu
from jax.sharding import PartitionSpec as P


EPS = 1e-06
LANES = 128
VMEM = pl.BlockSpec(memory_space=pltpu.VMEM)
FLOPS = 3_000_000_000
STAGE_FLOPS = 10_000_000_000


def swap_cores(block):
    return lax.ppermute(block, "tm", [(0, 1), (1, 0)])


def near_rows(block, distance):
    rows = lax.axis_size("rows")
    route = []
    for row in range(rows):
        down, up = row + distance, row - distance
        route.append((2 * row, 2 * down if down < rows else 2 * row + 1))
        route.append((2 * row + 1, 2 * up + 1 if up >= 0 else 2 * row))
    return lax.ppermute(block, ("rows", "tm"), route)


def slot_valid(slot):
    side = 1 - 2 * lax.axis_index("tm")
    at = lax.axis_index("rows") + slot * side
    return jnp.where((at >= 0) & (at < lax.axis_size("rows")), 1.0, 0.0)


def normed(floats, half_gain, channels, valid):
    mean = jnp.sum(floats * floats, axis=-1, keepdims=True) * (1.0 / channels)
    half = floats * (lax.rsqrt(mean + EPS) * valid) * half_gain
    return half + half * jnp.tanh(half)


def packing(channels):
    whole = channels // LANES * LANES
    rest = channels - whole
    return whole, rest, LANES // rest


def packed_plane(packed, frames, frame, place, channels):
    _, rest, count = packing(channels)
    low = packed[frame].astype(jnp.float32)
    high = packed[frames + lax.div(frame, count)].astype(jnp.float32)
    if place:
        high = pltpu.roll(high, LANES - place * rest, 1)
    lane = lax.broadcasted_iota(jnp.int32, high.shape, 1)
    return jnp.concatenate([low, jnp.where(lane < rest, high, 0.0)], axis=1)


def widened(plane, lanes):
    pad = jnp.zeros((plane.shape[0], lanes - plane.shape[1]), plane.dtype)
    return jnp.concatenate([plane, pad], axis=1)


def store_taps(taps, at, plane):
    edge = jnp.zeros((1, plane.shape[1]), plane.dtype)
    moved = (
        jnp.concatenate([edge, plane[:-1]], axis=0),
        plane,
        jnp.concatenate([plane[1:], edge], axis=0),
    )
    for tap, values in enumerate(moved):
        taps[(*at, tap)] = values.astype(jnp.bfloat16)


def slot_weights(weights, time_tap, row_taps, depth):
    core = lax.axis_index("tm")
    pad = jnp.zeros((depth - weights.shape[3], weights.shape[4]), weights.dtype)
    blocks = []
    for row_tap in row_taps:
        source = 2 * core + row_tap * (1 - 2 * core)
        for col_tap in range(3):
            blocks += [weights[time_tap, source, col_tap], pad]
    return jnp.concatenate(blocks, axis=0)


def causal(row_taps, planes, weights, total, base=None):
    slots, frames, cols, channels = total.shape
    for time_tap in (2, 1, 0):
        skip = 2 - time_tap
        pieces = []
        for refs in planes:
            for col_tap in range(3):
                parts = [ref[0, 0 : frames - skip, col_tap] for ref in refs]
                part = parts[0] if slots == 1 else jnp.concatenate(parts, axis=0)
                pieces.append(part.reshape(-1, part.shape[-1]))
        product = jnp.dot(
            jnp.concatenate(pieces, axis=-1),
            slot_weights(weights, time_tap, row_taps, pieces[0].shape[-1]),
            preferred_element_type=jnp.float32,
        ).reshape(slots, frames - skip, cols, channels)
        if skip == 0:
            total[...] = product if base is None else base[...] + product
        else:
            total[:, skip:] += product


def peak_of(plane):
    return jnp.max(jnp.abs(plane), axis=0, keepdims=True)


def rounded(values):
    return values.astype(jnp.bfloat16).astype(jnp.float32)


def stage_kernel(latent, staged):
    staged[...] = latent[...]


def join_kernel(mine, other, packed):
    frames, _, _, channels = mine.shape
    whole, _, count = packing(channels)
    clip_frames = 2 * frames
    first_core = lax.axis_index("tm") == 0
    planes = []
    for frame in range(clip_frames):
        near, far = (mine, other) if frame < frames else (other, mine)
        planes.append(jnp.where(first_core, near[frame % frames, 0], far[frame % frames, 0]))
    for frame, plane in enumerate(planes):
        packed[frame] = plane[:, :whole]
    for at in range(clip_frames // count):
        parts = [plane[:, whole:] for plane in planes[at * count : (at + 1) * count]]
        packed[clip_frames + at] = jnp.concatenate(parts, axis=1)


def own_kernel(own, gain_a, gain_b, weights, part_1, part_0, peak, half_a, half_b, taps):
    lanes = taps.shape[-1]
    channels = gain_a.shape[0]
    for gain, out in ((gain_a, half_a), (gain_b, half_b)):
        out[...] = widened(gain[...].reshape(1, -1).astype(jnp.float32) * 0.5, lanes)
    peak[...] = store_first(own, half_a, channels, 1.0, taps)
    causal((2,), ([taps],), weights, part_1)
    causal((1,), ([taps],), weights, part_0)


def store_first(packed, half_gain, channels, valid, taps):
    frames, lanes = taps.shape[1], taps.shape[-1]
    count = packing(channels)[2]
    top = jnp.zeros((1, lanes), jnp.float32)
    for frame in range(frames):
        plane = packed_plane(packed, frames, frame, frame % count, channels)
        first = normed(plane, half_gain[...], channels, valid)
        store_taps(taps, (0, frame), first)
        top = jnp.maximum(top, peak_of(first))
    return top


def store_second(total, half_gain, valid, taps, plain=None):
    frames, lanes = taps.shape[1], taps.shape[-1]
    top = jnp.zeros((1, lanes), jnp.float32)
    for frame in range(frames):
        hidden = widened(rounded(total[0, frame]), lanes)
        value = normed(hidden, half_gain[...], total.shape[-1], valid)
        store_taps(taps, (0, frame), value)
        if plain is not None:
            plain[frame] = value.astype(jnp.bfloat16)
        top = jnp.maximum(top, peak_of(value))
    return top


def near_kernel(
    near_1, near_2, part_1, half_a, half_b, weights, peak_in,
    near_taps, second_taps, second, part_2, peaks, outer_taps, total,
):
    channels = total.shape[-1]
    store_first(near_2, half_a, channels, slot_valid(-2), outer_taps)
    top = store_first(near_1, half_a, channels, slot_valid(-1), near_taps)
    peaks[0:1] = jnp.maximum(peak_in[...], top)
    causal((0, 1), ([outer_taps], [near_taps]), weights, total, part_1)
    causal((1, 2), ([outer_taps], [near_taps]), weights, part_2)
    peaks[1:2] = store_second(total, half_b, slot_valid(-1), second_taps, second)


def middle_kernel(
    far_1, near_3, near_taps, part_0, part_2, half_a, half_b, weights, peaks_in,
    taps_0, taps_2, second, peaks, far_taps, third_taps, total_0, total_2,
):
    channels = total_0.shape[-1]
    top = store_first(far_1, half_a, channels, slot_valid(1), far_taps)
    peaks[0:1] = jnp.maximum(peaks_in[0:1], top)
    store_first(near_3, half_a, channels, slot_valid(-3), third_taps)
    causal((0,), ([third_taps],), weights, total_2, part_2)
    causal((0, 2), ([near_taps], [far_taps]), weights, total_0, part_0)
    store_second(total_2, half_b, slot_valid(-2), taps_2, second)
    top = store_second(total_0, half_b, 1.0, taps_0)
    peaks[1:2] = jnp.maximum(peaks_in[1:2], top)


def merge(latents, slots, total, merged, top):
    out_frames = merged.shape[1]
    frames, _, channels = total.shape[1:]
    count = packing(channels)[2]
    core = lax.axis_index("tm")
    for place in range(frames):
        frame = lax.rem(core * out_frames + place, frames)
        for at, (latent, slot) in enumerate(zip(latents, slots)):
            plane = packed_plane(latent, frames, frame, place % count, channels)[:, :channels]
            value = (plane + total[at, frame]) * slot_valid(slot)
            top = jnp.maximum(top, peak_of(value))
            if place < out_frames:
                merged[at, place] = value.astype(jnp.bfloat16)
    return top


def inner_kernel(
    near_1, own, taps_2, taps_1, taps_0, second_far, weights, peaks_in,
    far_taps, merged, peaks, total,
):
    frames, _, channels = total.shape[1:]
    top = peaks_in[1:2]
    for frame in range(frames):
        value = second_far[frame].astype(jnp.float32)
        store_taps(far_taps, (0, frame), value)
        top = jnp.maximum(top, peak_of(value))
    peaks[0:1] = rounded(peaks_in[0:1])[:, :channels]
    peaks[1:2] = rounded(top)[:, :channels]
    causal((0, 1, 2), ([taps_2, taps_1], [taps_1, taps_0], [taps_0, far_taps]), weights, total)
    zero = jnp.zeros((1, channels), jnp.float32)
    peaks[2:3] = merge((near_1, own), (-1, 0), total, merged, zero)


def far_kernel(
    far_1, taps_0, far_taps, second_far, weights, peaks_in, merged, peaks, outer_taps, total
):
    for frame in range(total.shape[1]):
        store_taps(outer_taps, (0, frame), second_far[frame].astype(jnp.float32))
    causal((0, 1, 2), ([taps_0], [far_taps], [outer_taps]), weights, total)
    peaks[0:2] = peaks_in[0:2]
    peaks[2:3] = rounded(merge((far_1,), (1,), total, merged, peaks_in[2:3]))


def up_kernel(inner, outer, conv_up, decoded):
    frames, cols, _ = inner.shape[1:]
    first_core = lax.axis_index("tm") == 0
    out_channels = conv_up.shape[2]
    wide_cols = 2 * cols
    spread = jnp.where(
        lax.broadcasted_iota(jnp.int32, (wide_cols, cols), 0) // 2
        == lax.broadcasted_iota(jnp.int32, (wide_cols, cols), 1),
        1.0,
        0.0,
    ).astype(jnp.bfloat16)
    col = lax.broadcasted_iota(jnp.int32, (out_channels, wide_cols), 1)
    contract = (((1,), (1,)), ((), ()))
    sources = ((0, 1, 1), (1, 1, 2))
    for frame in range(frames):
        near, far = inner[0, frame], outer[0, frame]
        merged = (
            jnp.where(first_core, near, far),
            inner[1, frame],
            jnp.where(first_core, far, near),
        )
        wide = [
            jnp.dot(spread, row, preferred_element_type=jnp.float32).astype(jnp.bfloat16)
            for row in merged
        ]
        for half in range(2):
            sums = []
            for col_tap in range(3):
                total = None
                for row_tap in range(3):
                    term = lax.dot_general(
                        conv_up[row_tap, col_tap],
                        wide[sources[half][row_tap]],
                        contract,
                        preferred_element_type=jnp.float32,
                    )
                    total = term if total is None else total + term
                sums.append(total)
            left = jnp.where(col == 0, 0.0, pltpu.roll(sums[0], 1, 1))
            right = jnp.where(col == wide_cols - 1, 0.0, pltpu.roll(sums[2], wide_cols - 1, 1))
            decoded[frame, half] = (left + sums[1] + right).astype(jnp.bfloat16)


def peak_rounds(rows):
    bits = [1 << bit for bit in range(1, rows.bit_length() - 1)]
    rounds = []
    while bits:
        now, bits = bits[:2], bits[2:]
        rounds.append(now if len(now) == 1 else [now[0], now[1], now[0] | now[1]])
    return rounds


def group_peaks(peaks):
    rows = lax.axis_size("rows")
    for flips in peak_rounds(rows):
        arrived = []
        for flip in flips:
            arrived.append(lax.ppermute(peaks, "rows", [(r, r ^ flip) for r in range(rows)]))
        peaks = functools.reduce(jnp.maximum, arrived, peaks)
    return peaks


def per_device(latent, gain_first, conv_first, gain_second, conv_second, conv_up):
    frames, _, cols, channels = latent.shape
    clip_frames = lax.axis_size("tm") * frames
    lanes = -(-channels // LANES) * LANES
    bf16, f32 = jnp.bfloat16, jnp.float32
    taps_shape = (clip_frames, 3, cols, lanes)
    peaks_shape = jax.ShapeDtypeStruct((3, channels), f32)
    wide_peaks = jax.ShapeDtypeStruct((2, lanes), f32)
    row_shape = jax.ShapeDtypeStruct((1, lanes), f32)
    packed = clip_frames // packing(channels)[2] + clip_frames

    def call(kernel, outs, scratch, flops, *operands):
        return pl.pallas_call(
            kernel,
            out_shape=outs,
            in_specs=[VMEM] * len(operands),
            out_specs=jax.tree.map(lambda _: VMEM, outs),
            scratch_shapes=scratch,
            compiler_params=pltpu.CompilerParams(vmem_limit_bytes=16 << 20),
            cost_estimate=pl.CostEstimate(flops=flops, bytes_accessed=1 << 20, transcendentals=0),
        )(*operands)

    def totals(slots):
        return pltpu.VMEM((slots, clip_frames, cols, channels), f32)

    other = swap_cores(latent)
    mine = call(stage_kernel, jax.ShapeDtypeStruct(latent.shape, bf16), [], STAGE_FLOPS, latent)
    own = call(
        join_kernel, jax.ShapeDtypeStruct((packed, cols, LANES), bf16), [], FLOPS, mine, other
    )
    nears = []
    for distance in (1, 2, 3):
        nears.append(near_rows(own, distance))
    near_1, near_2, near_3 = nears
    taps_struct = jax.ShapeDtypeStruct((1, *taps_shape), bf16)
    taps_scratch = pltpu.VMEM((1, *taps_shape), bf16)
    plain = jax.ShapeDtypeStruct((clip_frames, cols, lanes), bf16)
    part = jax.ShapeDtypeStruct((1, clip_frames, cols, channels), f32)
    part_1, part_0, peak, half_a, half_b = call(
        own_kernel,
        (part, part, row_shape, row_shape, row_shape),
        [taps_scratch],
        FLOPS,
        own,
        gain_first,
        gain_second,
        conv_first,
    )
    near_1, part_1 = lax.optimization_barrier((near_1, part_1))
    far_1 = swap_cores(near_1)
    near_taps, taps_1, second_1, part_2, peaks = call(
        near_kernel,
        (taps_struct, taps_struct, plain, part, wide_peaks),
        [taps_scratch, totals(1)],
        FLOPS,
        near_1,
        near_2,
        part_1,
        half_a,
        half_b,
        conv_first,
        peak,
    )
    second_far_1 = swap_cores(second_1)
    taps_0, taps_2, second_2, peaks = call(
        middle_kernel,
        (taps_struct, taps_struct, plain, wide_peaks),
        [taps_scratch, taps_scratch, totals(1), totals(1)],
        FLOPS // 4,
        far_1,
        near_3,
        near_taps,
        part_0,
        part_2,
        half_a,
        half_b,
        conv_first,
        peaks,
    )
    second_far_2 = swap_cores(second_2)
    far_taps, merged, peaks = call(
        inner_kernel,
        (
            taps_struct,
            jax.ShapeDtypeStruct((2, frames, cols, channels), bf16),
            peaks_shape,
        ),
        [totals(2)],
        FLOPS,
        near_1,
        own,
        taps_2,
        taps_1,
        taps_0,
        second_far_1,
        conv_second,
        peaks,
    )
    merged_far, peaks = call(
        far_kernel,
        (jax.ShapeDtypeStruct((1, frames, cols, channels), bf16), peaks_shape),
        [taps_scratch, totals(1)],
        FLOPS,
        far_1,
        taps_0,
        far_taps,
        second_far_2,
        conv_second,
        peaks,
    )
    peaks = group_peaks(peaks)
    decoded = call(
        up_kernel,
        jax.ShapeDtypeStruct((frames, 2, conv_up.shape[2], 2 * cols), bf16),
        [],
        FLOPS,
        merged,
        merged_far,
        conv_up,
    )
    return decoded, peaks


def solution(mesh):
    return jax.shard_map(
        per_device,
        mesh=mesh,
        in_specs=(P(("clip", "tm"), "rows", None, None), P(), P(), P(), P(), P()),
        out_specs=(P(("clip", "tm"), "rows", None, None), P("clip", None)),
        check_vma=False,
    )
```

```python
import functools

import jax
import jax.numpy as jnp
from jax import lax
from jax.experimental import pallas as pl
from jax.experimental.pallas import tpu as pltpu
from jax.sharding import PartitionSpec as P


EPS = 1e-06
LANES = 128
PEAK_ROWS = 16
VMEM = pl.BlockSpec(memory_space=pltpu.VMEM)
FLOPS = 3_000_000_000
STAGE_FLOPS = 10_000_000_000


def swap_cores(block):
    return lax.ppermute(block, "tm", [(0, 1), (1, 0)])


def near_rows(block, distance):
    rows = lax.axis_size("rows")
    route = []
    for row in range(rows):
        down, up = row + distance, row - distance
        route.append((2 * row, 2 * down if down < rows else 2 * row + 1))
        route.append((2 * row + 1, 2 * up + 1 if up >= 0 else 2 * row))
    return lax.ppermute(block, ("rows", "tm"), route)


def slot_valid(slot):
    side = 1 - 2 * lax.axis_index("tm")
    at = lax.axis_index("rows") + slot * side
    return jnp.where((at >= 0) & (at < lax.axis_size("rows")), 1.0, 0.0)


def normed(floats, half_gain, channels, valid):
    mean = jnp.sum(floats * floats, axis=-1, keepdims=True) * (1.0 / channels)
    half = floats * (lax.rsqrt(mean + EPS) * valid) * half_gain
    return half + half * jnp.tanh(half)


def packing(channels):
    whole = channels // LANES * LANES
    rest = channels - whole
    return whole, rest, LANES // rest


def packed_plane(packed, frames, frame, place, channels):
    _, rest, count = packing(channels)
    low = packed[frame].astype(jnp.float32)
    high = packed[frames + lax.div(frame, count)].astype(jnp.float32)
    if place:
        high = pltpu.roll(high, LANES - place * rest, 1)
    lane = lax.broadcasted_iota(jnp.int32, high.shape, 1)
    return jnp.concatenate([low, jnp.where(lane < rest, high, 0.0)], axis=1)


def widened(plane, lanes):
    pad = jnp.zeros((plane.shape[0], lanes - plane.shape[1]), plane.dtype)
    return jnp.concatenate([plane, pad], axis=1)


def store_taps(taps, at, plane):
    edge = jnp.zeros((1, plane.shape[1]), plane.dtype)
    moved = (
        jnp.concatenate([edge, plane[:-1]], axis=0),
        plane,
        jnp.concatenate([plane[1:], edge], axis=0),
    )
    for tap, values in enumerate(moved):
        taps[(*at, tap)] = values.astype(jnp.bfloat16)


def slot_weights(weights, time_tap, row_taps, depth):
    core = lax.axis_index("tm")
    pad = jnp.zeros((depth - weights.shape[3], weights.shape[4]), weights.dtype)
    blocks = []
    for row_tap in row_taps:
        source = 2 * core + row_tap * (1 - 2 * core)
        for col_tap in range(3):
            blocks += [weights[time_tap, source, col_tap], pad]
    return jnp.concatenate(blocks, axis=0)


def causal(row_taps, planes, weights, total, base=None):
    slots, frames, cols, channels = total.shape
    for time_tap in (2, 1, 0):
        skip = 2 - time_tap
        pieces = []
        for refs in planes:
            for col_tap in range(3):
                parts = [ref[0, 0 : frames - skip, col_tap] for ref in refs]
                part = parts[0] if slots == 1 else jnp.concatenate(parts, axis=0)
                pieces.append(part.reshape(-1, part.shape[-1]))
        product = jnp.dot(
            jnp.concatenate(pieces, axis=-1),
            slot_weights(weights, time_tap, row_taps, pieces[0].shape[-1]),
            preferred_element_type=jnp.float32,
        ).reshape(slots, frames - skip, cols, channels)
        if skip == 0:
            total[...] = product if base is None else base[...] + product
        else:
            total[:, skip:] += product


def peak_of(plane):
    return jnp.max(jnp.abs(plane), axis=0, keepdims=True)


def rounded(values):
    return values.astype(jnp.bfloat16).astype(jnp.float32)


def stage_kernel(latent, staged):
    staged[...] = latent[...]


def join_kernel(mine, other, packed):
    frames, _, _, channels = mine.shape
    whole, _, count = packing(channels)
    clip_frames = 2 * frames
    first_core = lax.axis_index("tm") == 0
    planes = []
    for frame in range(clip_frames):
        near, far = (mine, other) if frame < frames else (other, mine)
        planes.append(jnp.where(first_core, near[frame % frames, 0], far[frame % frames, 0]))
    for frame, plane in enumerate(planes):
        packed[frame] = plane[:, :whole]
    for at in range(clip_frames // count):
        parts = [plane[:, whole:] for plane in planes[at * count : (at + 1) * count]]
        packed[clip_frames + at] = jnp.concatenate(parts, axis=1)


def own_kernel(own, gain_a, gain_b, weights, part_1, part_0, peak, half_a, half_b, taps):
    lanes = taps.shape[-1]
    channels = gain_a.shape[0]
    for gain, out in ((gain_a, half_a), (gain_b, half_b)):
        out[...] = widened(gain[...].reshape(1, -1).astype(jnp.float32) * 0.5, lanes)
    peak[...] = store_first(own, half_a, channels, 1.0, taps)
    causal((2,), ([taps],), weights, part_1)
    causal((1,), ([taps],), weights, part_0)


def store_first(packed, half_gain, channels, valid, taps):
    frames, lanes = taps.shape[1], taps.shape[-1]
    count = packing(channels)[2]
    top = jnp.zeros((1, lanes), jnp.float32)
    for frame in range(frames):
        plane = packed_plane(packed, frames, frame, frame % count, channels)
        first = normed(plane, half_gain[...], channels, valid)
        store_taps(taps, (0, frame), first)
        top = jnp.maximum(top, peak_of(first))
    return top


def store_second(total, half_gain, valid, taps, plain=None):
    frames, lanes = taps.shape[1], taps.shape[-1]
    top = jnp.zeros((1, lanes), jnp.float32)
    for frame in range(frames):
        hidden = widened(rounded(total[0, frame]), lanes)
        value = normed(hidden, half_gain[...], total.shape[-1], valid)
        store_taps(taps, (0, frame), value)
        if plain is not None:
            plain[frame] = value.astype(jnp.bfloat16)
        top = jnp.maximum(top, peak_of(value))
    return top


def near_kernel(
    near_1, near_2, part_1, half_a, half_b, weights, peak_in,
    near_taps, second_taps, second, part_2, peaks, outer_taps, total,
):
    channels = total.shape[-1]
    store_first(near_2, half_a, channels, slot_valid(-2), outer_taps)
    top = store_first(near_1, half_a, channels, slot_valid(-1), near_taps)
    peaks[0:1] = jnp.maximum(peak_in[...], top)
    causal((0, 1), ([outer_taps], [near_taps]), weights, total, part_1)
    causal((1, 2), ([outer_taps], [near_taps]), weights, part_2)
    peaks[1:2] = store_second(total, half_b, slot_valid(-1), second_taps, second)


def middle_kernel(
    far_1, near_3, near_taps, part_0, part_2, half_a, half_b, weights, peaks_in,
    taps_0, taps_2, peaks, far_taps, third_taps, total_0, total_2,
):
    channels = total_0.shape[-1]
    top = store_first(far_1, half_a, channels, slot_valid(1), far_taps)
    peaks[0:1] = jnp.maximum(peaks_in[0:1], top)
    store_first(near_3, half_a, channels, slot_valid(-3), third_taps)
    causal((0,), ([third_taps],), weights, total_2, part_2)
    causal((0, 2), ([near_taps], [far_taps]), weights, total_0, part_0)
    store_second(total_2, half_b, slot_valid(-2), taps_2)
    top = store_second(total_0, half_b, 1.0, taps_0)
    peaks[1:2] = jnp.maximum(peaks_in[1:2], top)


def merge(latent, slot, total, merged):
    frames, _, channels = total.shape[1:]
    count = packing(channels)[2]
    top = jnp.zeros((1, channels), jnp.float32)
    for frame in range(frames):
        plane = packed_plane(latent, frames, frame, frame % count, channels)[:, :channels]
        value = (plane + total[0, frame]) * slot_valid(slot)
        top = jnp.maximum(top, peak_of(value))
        merged[frame] = value.astype(jnp.bfloat16)
    return top


def side_kernel(near_1, taps_2, taps_1, taps_0, weights, merged, sent, total):
    frames, cols, _ = merged.shape
    count = frames // 2
    causal((0, 1, 2), ([taps_2], [taps_1], [taps_0]), weights, total)
    top = merge(near_1, -1, total, merged)
    other = 1 - lax.axis_index("tm")
    for place in range(count):
        sent[place * cols : (place + 1) * cols] = merged[other * count + place]
    rest = sent.shape[0] - count * cols
    sent[count * cols :] = jnp.broadcast_to(top, (rest, top.shape[1])).astype(jnp.bfloat16)


def inner_kernel(own, taps_1, taps_0, second_far, weights, peaks_in, merged, peaks, far_taps, total):
    frames, _, channels = total.shape[1:]
    top = peaks_in[1:2]
    for frame in range(frames):
        value = second_far[frame].astype(jnp.float32)
        store_taps(far_taps, (0, frame), value)
        top = jnp.maximum(top, peak_of(value))
    peaks[0:1] = rounded(peaks_in[0:1])[:, :channels]
    peaks[1:2] = rounded(top)[:, :channels]
    causal((0, 1, 2), ([taps_1], [taps_0], [far_taps]), weights, total)
    peaks[2:3] = rounded(merge(own, 0, total, merged))


def up_kernel(near_merged, own_merged, far_merged, conv_up, decoded):
    frames, _, out_channels, wide_cols = decoded.shape
    cols = own_merged.shape[1]
    core = lax.axis_index("tm")
    spread = jnp.where(
        lax.broadcasted_iota(jnp.int32, (wide_cols, cols), 0) // 2
        == lax.broadcasted_iota(jnp.int32, (wide_cols, cols), 1),
        1.0,
        0.0,
    ).astype(jnp.bfloat16)
    col = lax.broadcasted_iota(jnp.int32, (out_channels, wide_cols), 1)

    def products(row, row_taps):
        wide = jnp.dot(spread, row, preferred_element_type=jnp.float32).astype(jnp.bfloat16)
        taps = conv_up[row_taps[0] : row_taps[-1] + 1]
        result = lax.dot_general(
            taps.reshape(-1, taps.shape[-1]),
            wide,
            (((1,), (1,)), ((), ())),
            preferred_element_type=jnp.float32,
        )
        return result.reshape(len(row_taps), 3, out_channels, wide_cols)

    for place in range(frames):
        frame = core * frames + place
        near, far = near_merged[frame], far_merged[place * cols : (place + 1) * cols]
        above = products(jnp.where(core == 0, near, far), (0,))
        below = products(jnp.where(core == 0, far, near), (2,))
        middle = products(own_merged[frame], (0, 1, 2))
        for half in range(2):
            sums = []
            for tap in range(3):
                if half == 0:
                    sums.append(above[0, tap] + middle[1, tap] + middle[2, tap])
                else:
                    sums.append(middle[0, tap] + middle[1, tap] + below[0, tap])
            left = jnp.where(col == 0, 0.0, pltpu.roll(sums[0], 1, 1))
            right = jnp.where(col == wide_cols - 1, 0.0, pltpu.roll(sums[2], wide_cols - 1, 1))
            decoded[place, half] = (left + sums[1] + right).astype(jnp.bfloat16)


def peak_rounds(rows):
    bits = [1 << bit for bit in range(1, rows.bit_length() - 1)]
    rounds = []
    while bits:
        now, bits = bits[:2], bits[2:]
        rounds.append(now if len(now) == 1 else [now[0], now[1], now[0] | now[1]])
    return rounds


def group_peaks(peaks):
    rows = lax.axis_size("rows")
    for flips in peak_rounds(rows):
        arrived = []
        for flip in flips:
            arrived.append(lax.ppermute(peaks, "rows", [(r, r ^ flip) for r in range(rows)]))
        peaks = functools.reduce(jnp.maximum, arrived, peaks)
    return peaks


def per_device(latent, gain_first, conv_first, gain_second, conv_second, conv_up):
    frames, _, cols, channels = latent.shape
    clip_frames = lax.axis_size("tm") * frames
    lanes = -(-channels // LANES) * LANES
    bf16, f32 = jnp.bfloat16, jnp.float32
    taps_shape = (clip_frames, 3, cols, lanes)
    peaks_shape = jax.ShapeDtypeStruct((3, channels), f32)
    wide_peaks = jax.ShapeDtypeStruct((2, lanes), f32)
    row_shape = jax.ShapeDtypeStruct((1, lanes), f32)
    packed = clip_frames // packing(channels)[2] + clip_frames

    def call(kernel, outs, scratch, flops, *operands):
        return pl.pallas_call(
            kernel,
            out_shape=outs,
            in_specs=[VMEM] * len(operands),
            out_specs=jax.tree.map(lambda _: VMEM, outs),
            scratch_shapes=scratch,
            compiler_params=pltpu.CompilerParams(vmem_limit_bytes=16 << 20),
            cost_estimate=pl.CostEstimate(flops=flops, bytes_accessed=1 << 20, transcendentals=0),
        )(*operands)

    def totals(slots):
        return pltpu.VMEM((slots, clip_frames, cols, channels), f32)

    other = swap_cores(latent)
    mine = call(stage_kernel, jax.ShapeDtypeStruct(latent.shape, bf16), [], STAGE_FLOPS, latent)
    own = call(
        join_kernel, jax.ShapeDtypeStruct((packed, cols, LANES), bf16), [], FLOPS, mine, other
    )
    nears = []
    for distance in (1, 2, 3):
        nears.append(near_rows(own, distance))
    near_1, near_2, near_3 = nears
    taps_struct = jax.ShapeDtypeStruct((1, *taps_shape), bf16)
    taps_scratch = pltpu.VMEM((1, *taps_shape), bf16)
    plain = jax.ShapeDtypeStruct((clip_frames, cols, lanes), bf16)
    part = jax.ShapeDtypeStruct((1, clip_frames, cols, channels), f32)
    part_1, part_0, peak, half_a, half_b = call(
        own_kernel,
        (part, part, row_shape, row_shape, row_shape),
        [taps_scratch],
        FLOPS,
        own,
        gain_first,
        gain_second,
        conv_first,
    )
    near_1, part_1 = lax.optimization_barrier((near_1, part_1))
    far_1 = swap_cores(near_1)
    near_taps, taps_1, second_1, part_2, peaks = call(
        near_kernel,
        (taps_struct, taps_struct, plain, part, wide_peaks),
        [taps_scratch, totals(1)],
        FLOPS,
        near_1,
        near_2,
        part_1,
        half_a,
        half_b,
        conv_first,
        peak,
    )
    second_far_1 = swap_cores(second_1)
    taps_0, taps_2, peaks = call(
        middle_kernel,
        (taps_struct, taps_struct, wide_peaks),
        [taps_scratch, taps_scratch, totals(1), totals(1)],
        FLOPS // 4,
        far_1,
        near_3,
        near_taps,
        part_0,
        part_2,
        half_a,
        half_b,
        conv_first,
        peaks,
    )
    merged_struct = jax.ShapeDtypeStruct((clip_frames, cols, channels), bf16)
    merged_near, sent = call(
        side_kernel,
        (
            merged_struct,
            jax.ShapeDtypeStruct((frames * cols + PEAK_ROWS, channels), bf16),
        ),
        [totals(1)],
        FLOPS,
        near_1,
        taps_2,
        taps_1,
        taps_0,
        conv_second,
    )
    merged_far = swap_cores(sent)
    merged_own, peaks = call(
        inner_kernel,
        (merged_struct, peaks_shape),
        [taps_scratch, totals(1)],
        FLOPS,
        own,
        taps_1,
        taps_0,
        second_far_1,
        conv_second,
        peaks,
    )
    sides = jnp.maximum(sent[frames * cols], merged_far[frames * cols]).astype(f32)
    peaks = jnp.maximum(peaks, jnp.stack([jnp.zeros_like(sides)] * 2 + [sides]))
    peaks = group_peaks(peaks)
    decoded = call(
        up_kernel,
        jax.ShapeDtypeStruct((frames, 2, conv_up.shape[2], 2 * cols), bf16),
        [],
        FLOPS,
        merged_near,
        merged_own,
        merged_far,
        conv_up,
    )
    return decoded, peaks


def solution(mesh):
    return jax.shard_map(
        per_device,
        mesh=mesh,
        in_specs=(P(("clip", "tm"), "rows", None, None), P(), P(), P(), P(), P()),
        out_specs=(P(("clip", "tm"), "rows", None, None), P("clip", None)),
        check_vma=False,
    )
```

```python
import functools

import jax
import jax.numpy as jnp
from jax import lax
from jax.experimental import pallas as pl
from jax.experimental.pallas import tpu as pltpu
from jax.sharding import PartitionSpec as P


EPS = 1e-06
LANES = 128
PEAK_ROWS = 16
VMEM = pl.BlockSpec(memory_space=pltpu.VMEM)
FLOPS = 3_000_000_000
STAGE_FLOPS = 10_000_000_000


def swap_cores(block):
    return lax.ppermute(block, "tm", [(0, 1), (1, 0)])


def near_rows(block, distance):
    rows = lax.axis_size("rows")
    route = []
    for row in range(rows):
        down, up = row + distance, row - distance
        route.append((2 * row, 2 * down if down < rows else 2 * row + 1))
        route.append((2 * row + 1, 2 * up + 1 if up >= 0 else 2 * row))
    return lax.ppermute(block, ("rows", "tm"), route)


def slot_valid(slot):
    side = 1 - 2 * lax.axis_index("tm")
    at = lax.axis_index("rows") + slot * side
    return jnp.where((at >= 0) & (at < lax.axis_size("rows")), 1.0, 0.0)


def normed(floats, half_gain, channels, valid):
    mean = jnp.sum(floats * floats, axis=-1, keepdims=True) * (1.0 / channels)
    half = floats * (lax.rsqrt(mean + EPS) * valid) * half_gain
    return half + half * jnp.tanh(half)


def packing(channels):
    whole = channels // LANES * LANES
    rest = channels - whole
    return whole, rest, LANES // rest


def packed_plane(packed, frames, frame, place, channels):
    _, rest, count = packing(channels)
    low = packed[frame].astype(jnp.float32)
    high = packed[frames + lax.div(frame, count)].astype(jnp.float32)
    if place:
        high = pltpu.roll(high, LANES - place * rest, 1)
    lane = lax.broadcasted_iota(jnp.int32, high.shape, 1)
    return jnp.concatenate([low, jnp.where(lane < rest, high, 0.0)], axis=1)


def widened(plane, lanes):
    pad = jnp.zeros((plane.shape[0], lanes - plane.shape[1]), plane.dtype)
    return jnp.concatenate([plane, pad], axis=1)


def store_taps(taps, at, plane):
    edge = jnp.zeros((1, plane.shape[1]), plane.dtype)
    moved = (
        jnp.concatenate([edge, plane[:-1]], axis=0),
        plane,
        jnp.concatenate([plane[1:], edge], axis=0),
    )
    for tap, values in enumerate(moved):
        taps[(*at, tap)] = values.astype(jnp.bfloat16)


def slot_weights(weights, time_tap, row_taps, depth):
    core = lax.axis_index("tm")
    pad = jnp.zeros((depth - weights.shape[3], weights.shape[4]), weights.dtype)
    blocks = []
    for row_tap in row_taps:
        source = 2 * core + row_tap * (1 - 2 * core)
        for col_tap in range(3):
            blocks += [weights[time_tap, source, col_tap], pad]
    return jnp.concatenate(blocks, axis=0)


def causal(row_taps, planes, weights, total, base=None):
    slots, frames, cols, channels = total.shape
    for time_tap in (2, 1, 0):
        skip = 2 - time_tap
        pieces = []
        for refs in planes:
            for col_tap in range(3):
                parts = [ref[0, 0 : frames - skip, col_tap] for ref in refs]
                part = parts[0] if slots == 1 else jnp.concatenate(parts, axis=0)
                pieces.append(part.reshape(-1, part.shape[-1]))
        product = jnp.dot(
            jnp.concatenate(pieces, axis=-1),
            slot_weights(weights, time_tap, row_taps, pieces[0].shape[-1]),
            preferred_element_type=jnp.float32,
        ).reshape(slots, frames - skip, cols, channels)
        if skip == 0:
            total[...] = product if base is None else base[...] + product
        else:
            total[:, skip:] += product


def peak_of(plane):
    return jnp.max(jnp.abs(plane), axis=0, keepdims=True)


def rounded(values):
    return values.astype(jnp.bfloat16).astype(jnp.float32)


def stage_kernel(latent, staged):
    staged[...] = latent[...]


def join_kernel(mine, other, packed):
    frames, _, _, channels = mine.shape
    whole, _, count = packing(channels)
    clip_frames = 2 * frames
    first_core = lax.axis_index("tm") == 0
    planes = []
    for frame in range(clip_frames):
        near, far = (mine, other) if frame < frames else (other, mine)
        planes.append(jnp.where(first_core, near[frame % frames, 0], far[frame % frames, 0]))
    for frame, plane in enumerate(planes):
        packed[frame] = plane[:, :whole]
    for at in range(clip_frames // count):
        parts = [plane[:, whole:] for plane in planes[at * count : (at + 1) * count]]
        packed[clip_frames + at] = jnp.concatenate(parts, axis=1)


def own_kernel(own, gain_a, gain_b, weights, part_1, part_0, peak, half_a, half_b, taps):
    lanes = taps.shape[-1]
    channels = gain_a.shape[0]
    for gain, out in ((gain_a, half_a), (gain_b, half_b)):
        out[...] = widened(gain[...].reshape(1, -1).astype(jnp.float32) * 0.5, lanes)
    peak[...] = store_first(own, half_a, channels, 1.0, taps)
    causal((2,), ([taps],), weights, part_1)
    causal((1,), ([taps],), weights, part_0)


def store_first(packed, half_gain, channels, valid, taps):
    frames, lanes = taps.shape[1], taps.shape[-1]
    count = packing(channels)[2]
    top = jnp.zeros((1, lanes), jnp.float32)
    for frame in range(frames):
        plane = packed_plane(packed, frames, frame, frame % count, channels)
        first = normed(plane, half_gain[...], channels, valid)
        store_taps(taps, (0, frame), first)
        top = jnp.maximum(top, peak_of(first))
    return top


def store_second(total, half_gain, valid, taps, plain=None):
    frames, lanes = taps.shape[1], taps.shape[-1]
    top = jnp.zeros((1, lanes), jnp.float32)
    for frame in range(frames):
        hidden = widened(rounded(total[0, frame]), lanes)
        value = normed(hidden, half_gain[...], total.shape[-1], valid)
        store_taps(taps, (0, frame), value)
        if plain is not None:
            plain[frame] = value.astype(jnp.bfloat16)
        top = jnp.maximum(top, peak_of(value))
    return top


def near_kernel(
    near_1, near_2, part_1, half_a, half_b, weights, peak_in,
    near_taps, second_taps, second, part_2, peaks, outer_taps, total,
):
    channels = total.shape[-1]
    store_first(near_2, half_a, channels, slot_valid(-2), outer_taps)
    top = store_first(near_1, half_a, channels, slot_valid(-1), near_taps)
    peaks[0:1] = jnp.maximum(peak_in[...], top)
    causal((0, 1), ([outer_taps], [near_taps]), weights, total, part_1)
    causal((1, 2), ([outer_taps], [near_taps]), weights, part_2)
    peaks[1:2] = store_second(total, half_b, slot_valid(-1), second_taps, second)


def middle_kernel(
    far_1, near_3, near_taps, part_0, part_2, half_a, half_b, weights, peaks_in,
    taps_0, taps_2, peaks, far_taps, third_taps, total_0, total_2,
):
    channels = total_0.shape[-1]
    top = store_first(far_1, half_a, channels, slot_valid(1), far_taps)
    peaks[0:1] = jnp.maximum(peaks_in[0:1], top)
    store_first(near_3, half_a, channels, slot_valid(-3), third_taps)
    causal((0,), ([third_taps],), weights, total_2, part_2)
    causal((0, 2), ([near_taps], [far_taps]), weights, total_0, part_0)
    store_second(total_2, half_b, slot_valid(-2), taps_2)
    top = store_second(total_0, half_b, 1.0, taps_0)
    peaks[1:2] = jnp.maximum(peaks_in[1:2], top)


def merge(latent, slot, total, merged):
    frames, _, channels = total.shape[1:]
    count = packing(channels)[2]
    top = jnp.zeros((1, channels), jnp.float32)
    for frame in range(frames):
        plane = packed_plane(latent, frames, frame, frame % count, channels)[:, :channels]
        value = (plane + total[0, frame]) * slot_valid(slot)
        top = jnp.maximum(top, peak_of(value))
        merged[frame] = value.astype(jnp.bfloat16)
    return top


def side_kernel(near_1, taps_2, taps_1, taps_0, weights, merged, sent, total):
    frames, cols, _ = merged.shape
    count = frames // 2
    causal((0, 1, 2), ([taps_2], [taps_1], [taps_0]), weights, total)
    top = merge(near_1, -1, total, merged)
    other = 1 - lax.axis_index("tm")
    for place in range(count):
        sent[place * cols : (place + 1) * cols] = merged[other * count + place]
    rest = sent.shape[0] - count * cols
    sent[count * cols :] = jnp.broadcast_to(top, (rest, top.shape[1])).astype(jnp.bfloat16)


def inner_kernel(own, taps_1, taps_0, second_far, weights, peaks_in, merged, peaks, far_taps, total):
    frames, _, channels = total.shape[1:]
    top = peaks_in[1:2]
    for frame in range(frames):
        value = second_far[frame].astype(jnp.float32)
        store_taps(far_taps, (0, frame), value)
        top = jnp.maximum(top, peak_of(value))
    peaks[0:1] = rounded(peaks_in[0:1])[:, :channels]
    peaks[1:2] = rounded(top)[:, :channels]
    causal((0, 1, 2), ([taps_1], [taps_0], [far_taps]), weights, total)
    peaks[2:3] = rounded(merge(own, 0, total, merged))


def up_kernel(near_merged, own_merged, far_merged, conv_up, decoded):
    frames, _, out_channels, wide_cols = decoded.shape
    cols = own_merged.shape[1]
    core = lax.axis_index("tm")
    spread = jnp.where(
        lax.broadcasted_iota(jnp.int32, (wide_cols, cols), 0) // 2
        == lax.broadcasted_iota(jnp.int32, (wide_cols, cols), 1),
        1.0,
        0.0,
    ).astype(jnp.bfloat16)
    col = lax.broadcasted_iota(jnp.int32, (out_channels, wide_cols), 1)

    def products(row, row_taps):
        wide = jnp.dot(spread, row, preferred_element_type=jnp.float32).astype(jnp.bfloat16)
        taps = conv_up[row_taps[0] : row_taps[-1] + 1]
        result = lax.dot_general(
            taps.reshape(-1, taps.shape[-1]),
            wide,
            (((1,), (1,)), ((), ())),
            preferred_element_type=jnp.float32,
        )
        return result.reshape(len(row_taps), 3, out_channels, wide_cols)

    for place in range(frames):
        frame = core * frames + place
        near, far = near_merged[frame], far_merged[place * cols : (place + 1) * cols]
        above = products(jnp.where(core == 0, near, far), (0,))
        below = products(jnp.where(core == 0, far, near), (2,))
        middle = products(own_merged[frame], (0, 1, 2))
        for half in range(2):
            sums = []
            for tap in range(3):
                if half == 0:
                    sums.append(above[0, tap] + middle[1, tap] + middle[2, tap])
                else:
                    sums.append(middle[0, tap] + middle[1, tap] + below[0, tap])
            left = jnp.where(col == 0, 0.0, pltpu.roll(sums[0], 1, 1))
            right = jnp.where(col == wide_cols - 1, 0.0, pltpu.roll(sums[2], wide_cols - 1, 1))
            decoded[place, half] = (left + sums[1] + right).astype(jnp.bfloat16)


def peak_rounds(rows):
    bits = [1 << bit for bit in range(1, rows.bit_length() - 1)]
    rounds = []
    while bits:
        now, bits = bits[:2], bits[2:]
        rounds.append(now if len(now) == 1 else [now[0], now[1], now[0] | now[1]])
    return rounds


def flipped(peaks, flip_0, flip_1):
    route = []
    for row in range(lax.axis_size("rows")):
        route.append((2 * row, 2 * (row ^ flip_0)))
        route.append((2 * row + 1, 2 * (row ^ flip_1) + 1))
    return lax.ppermute(peaks, ("rows", "tm"), route)


def group_peaks(peaks):
    for flips in peak_rounds(lax.axis_size("rows")):
        turns = [(flips[0], flips[2]), (flips[1], flips[0])] if len(flips) == 3 else [flips * 2]
        arrived = [peaks]
        for flip_0, flip_1 in turns:
            arrived.append(flipped(peaks, flip_0, flip_1))
        peaks = functools.reduce(jnp.maximum, arrived)
        if len(flips) == 3:
            peaks = jnp.maximum(peaks, swap_cores(peaks))
    return peaks


def per_device(latent, gain_first, conv_first, gain_second, conv_second, conv_up):
    frames, _, cols, channels = latent.shape
    clip_frames = lax.axis_size("tm") * frames
    lanes = -(-channels // LANES) * LANES
    bf16, f32 = jnp.bfloat16, jnp.float32
    taps_shape = (clip_frames, 3, cols, lanes)
    peaks_shape = jax.ShapeDtypeStruct((3, channels), f32)
    wide_peaks = jax.ShapeDtypeStruct((2, lanes), f32)
    row_shape = jax.ShapeDtypeStruct((1, lanes), f32)
    packed = clip_frames // packing(channels)[2] + clip_frames

    def call(kernel, outs, scratch, flops, *operands):
        return pl.pallas_call(
            kernel,
            out_shape=outs,
            in_specs=[VMEM] * len(operands),
            out_specs=jax.tree.map(lambda _: VMEM, outs),
            scratch_shapes=scratch,
            compiler_params=pltpu.CompilerParams(vmem_limit_bytes=16 << 20),
            cost_estimate=pl.CostEstimate(flops=flops, bytes_accessed=1 << 20, transcendentals=0),
        )(*operands)

    def totals(slots):
        return pltpu.VMEM((slots, clip_frames, cols, channels), f32)

    other = swap_cores(latent)
    mine = call(stage_kernel, jax.ShapeDtypeStruct(latent.shape, bf16), [], STAGE_FLOPS, latent)
    own = call(
        join_kernel, jax.ShapeDtypeStruct((packed, cols, LANES), bf16), [], FLOPS, mine, other
    )
    nears = []
    for distance in (1, 2, 3):
        nears.append(near_rows(own, distance))
    near_1, near_2, near_3 = nears
    taps_struct = jax.ShapeDtypeStruct((1, *taps_shape), bf16)
    taps_scratch = pltpu.VMEM((1, *taps_shape), bf16)
    plain = jax.ShapeDtypeStruct((clip_frames, cols, lanes), bf16)
    part = jax.ShapeDtypeStruct((1, clip_frames, cols, channels), f32)
    part_1, part_0, peak, half_a, half_b = call(
        own_kernel,
        (part, part, row_shape, row_shape, row_shape),
        [taps_scratch],
        FLOPS,
        own,
        gain_first,
        gain_second,
        conv_first,
    )
    near_1, part_1 = lax.optimization_barrier((near_1, part_1))
    far_1 = swap_cores(near_1)
    near_taps, taps_1, second_1, part_2, peaks = call(
        near_kernel,
        (taps_struct, taps_struct, plain, part, wide_peaks),
        [taps_scratch, totals(1)],
        FLOPS,
        near_1,
        near_2,
        part_1,
        half_a,
        half_b,
        conv_first,
        peak,
    )
    second_far_1 = swap_cores(second_1)
    taps_0, taps_2, peaks = call(
        middle_kernel,
        (taps_struct, taps_struct, wide_peaks),
        [taps_scratch, taps_scratch, totals(1), totals(1)],
        FLOPS // 4,
        far_1,
        near_3,
        near_taps,
        part_0,
        part_2,
        half_a,
        half_b,
        conv_first,
        peaks,
    )
    merged_struct = jax.ShapeDtypeStruct((clip_frames, cols, channels), bf16)
    merged_near, sent = call(
        side_kernel,
        (
            merged_struct,
            jax.ShapeDtypeStruct((frames * cols + PEAK_ROWS, channels), bf16),
        ),
        [totals(1)],
        FLOPS,
        near_1,
        taps_2,
        taps_1,
        taps_0,
        conv_second,
    )
    merged_far = swap_cores(sent)
    merged_own, peaks = call(
        inner_kernel,
        (merged_struct, peaks_shape),
        [taps_scratch, totals(1)],
        FLOPS,
        own,
        taps_1,
        taps_0,
        second_far_1,
        conv_second,
        peaks,
    )
    sides = jnp.maximum(sent[frames * cols], merged_far[frames * cols]).astype(f32)
    peaks = jnp.maximum(peaks, jnp.stack([jnp.zeros_like(sides)] * 2 + [sides]))
    peaks = group_peaks(peaks)
    decoded = call(
        up_kernel,
        jax.ShapeDtypeStruct((frames, 2, conv_up.shape[2], 2 * cols), bf16),
        [],
        FLOPS,
        merged_near,
        merged_own,
        merged_far,
        conv_up,
    )
    return decoded, peaks


def solution(mesh):
    return jax.shard_map(
        per_device,
        mesh=mesh,
        in_specs=(P(("clip", "tm"), "rows", None, None), P(), P(), P(), P(), P()),
        out_specs=(P(("clip", "tm"), "rows", None, None), P("clip", None)),
        check_vma=False,
    )
```
